256 devices in a mesh: cls: 4 (over y), dom: 64 (over z, x, core).
Axes of the slice: x: 4, y: 4, z: 8, core: 2. Of those that a mesh axis runs over, the one named last changes fastest.
Arguments:
- particles: bfloat16 [65536, 4096], P('dom', 'cls'), may hold values from -6 to 8
- candidates: int32 [65536, 2], P('dom'), may hold values from 0 to 63, all different within a row; in each aligned block of 1024 rows (0 to 1023, 1024 to 2047, ...) at most 64 rows name the same one
- defocus: int32 [65536], P('dom'), may hold values from 0 to 31
- ctf_table: float32 [32, 4096], P(None, 'cls'), may hold values from -1 to 1
- references: bfloat16 [256, 4096], P('dom', 'cls'), may hold values from -5 to 5
- rotations: bfloat16 [64, 64, 64], replicated, may hold values from -0.4 to 1.1
Outputs:
- class_sums: bfloat16 [256, 4096], P('dom', 'cls')
- class_weights: float32 [256, 4096], P('dom', 'cls')
- log_evidence: float32 [65536], P('dom')
The draws below stay inside these ranges and needn't reach their ends.
Inputs may be any that keep to these rules, and one draw needn't show every extreme that they name: The two candidates of a particle differ; among the 1024 particles of one index of dom no group is named by more than 64 entries, a bound that some block reaches.
All inputs are finite; a program needn't handle non-finite values.
Results may differ from the reference program's by a relative error of at most 0.0054.
Values may be sent and summed in bfloat16 or wider, within the bound.
A program may use at most 128 MiB of HBM per device.

```python
import math
import jax
import jax.numpy as jnp
import numpy as np
from jax import lax

CYCLES = 64
ANG = 64
ROT = 64
CPG = 4
DEF = 32
TOK_DEV = 1024
PIX = 4096
CLASSES = 256
PARTS_SIZE = 65536
CAP = 64
N_DOM = 64


def draw_particles(key, part):
    noise_key = jax.random.fold_in(key, 11)
    values = jnp.clip(jax.random.normal(noise_key, (PARTS_SIZE, PIX), jnp.float32), -6.0, 6.0)
    return values.astype(jnp.bfloat16)


def draw_references(key, part):
    noise_key = jax.random.fold_in(key, 21)
    values = jnp.clip(jax.random.normal(noise_key, (CLASSES, PIX), jnp.float32), -5.0, 5.0)
    return values.astype(jnp.bfloat16)


def draw_ctf_table(key, part):
    noise_key = jax.random.fold_in(key, 31)
    values = jax.random.uniform(noise_key, (DEF, PIX), jnp.float32, -1.0, 1.0)
    return values


def draw_rotations(key, part):
    noise_key = jax.random.fold_in(key, 41)
    turn_ids = lax.broadcasted_iota(jnp.int32, (ROT, ANG, ANG), 0)
    target = lax.broadcasted_iota(jnp.int32, (ROT, ANG, ANG), 1)
    source = lax.broadcasted_iota(jnp.int32, (ROT, ANG, ANG), 2)
    offset = turn_ids * ANG // ROT
    hit = ((target - offset - source) % ANG == 0).astype(jnp.float32)
    noise = jnp.clip(jax.random.normal(noise_key, (ROT, ANG, ANG), jnp.float32), -4.0, 4.0)
    values = 0.7 * hit + noise * (0.35 / ANG ** 0.5)
    return values.astype(jnp.bfloat16)


def touch_ends(values, stream_key, smallest, high):
    dims = values.shape
    index_at = [jax.random.randint(jax.random.fold_in(stream_key, axis), (), 0, dims[axis]) for axis in range(len(dims))]
    values = values.at[tuple(index_at)].set(smallest)
    longest = dims.index(max(dims))
    index_at[longest] = (index_at[longest] + 1) % dims[longest]
    return values.at[tuple(index_at)].set(high)


def deal_out(rng, own, number, rows, number_of, top, limit, skew):
    sequence = jax.random.permutation(rng, number_of)
    heavy_load, usual = load_shares(number_of, rows * top, limit, skew, True), load_shares(number_of, rows * top, limit, skew, False)
    places = jnp.arange(number_of)

    def named(tallies, rotation):
        used = int((tallies > 0).sum())
        fixed = max(1, used // 4)
        moved = fixed + (places - fixed + rotation * (used - fixed)) % max(1, number_of - fixed)
        return jnp.zeros((number_of,), jnp.int32).at[sequence[jnp.where(places < fixed, places, moved)]].set(jnp.asarray(tallies, jnp.int32))

    tallies = jnp.where(number % 4 == 0, named(heavy_load, number // 4), named(usual, number - number // 4 - 1))
    mixed = jax.random.permutation(jax.random.fold_in(own, 3), number_of)
    giver, sink = mixed[0:number_of // 2 * 2:2], mixed[1:number_of // 2 * 2:2]
    margin = jnp.minimum(tallies[giver] - 1, limit - tallies[sink]) // 2
    margin = jnp.where((giver == sequence[0]) | (sink == sequence[0]) | (tallies[sink] == 0), 0, jnp.maximum(margin, 0))
    moved = jax.random.randint(jax.random.fold_in(own, 4), (number_of // 2,), 0, 1 << 20) % (margin + 1)
    tallies = tallies.at[giver].add(-moved).at[sink].add(moved)
    labels = jnp.searchsorted(jnp.cumsum(tallies), jnp.arange(rows * top), side="right").astype(jnp.int32)
    grid = labels.reshape(top, rows).T
    grid = grid[jax.random.permutation(jax.random.fold_in(own, 1), rows)]
    rotation = jax.random.randint(jax.random.fold_in(own, 2), (rows, 1), 0, top)
    return jnp.take_along_axis(grid, (jnp.arange(top)[None, :] + rotation) % top, axis=1)


def load_shares(number_of, total, limit, skew, full):
    loads = [(1 << 20) // math.isqrt(rank ** skew) + 1 for rank in range(1, number_of + 1)]
    largest = limit if full else min(limit, max(-(-total // number_of), total * loads[0] // sum(loads)))
    least = 1 if total - largest >= number_of - 1 else 0
    holding, rest = [largest] + [least] * (number_of - 1), total - largest - least * (number_of - 1)
    while rest > 0:
        free = [i for i in range(1, number_of) if holding[i] < largest] or [i for i in range(1, number_of) if holding[i] < limit]
        whole, remaining = sum([loads[i] for i in free]), rest
        for i in free:
            more = min(limit - holding[i], max(1, remaining * loads[i] // whole), rest)
            holding[i] = holding[i] + more
            rest = rest - more
    return np.array(holding)


def setup_inputs(seed: int = 0) -> dict:
    key_of = jax.random.split(jax.random.key(seed), 7)
    particles = draw_particles(jax.random.fold_in(key_of[6], 71), 0)
    candidates_keys = jax.random.split(jax.random.fold_in(key_of[1], 1), PARTS_SIZE // TOK_DEV)
    candidates_turns = jax.random.permutation(jax.random.fold_in(key_of[1], 3), PARTS_SIZE // TOK_DEV)
    candidates = jax.vmap(lambda own, number: deal_out(jax.random.fold_in(key_of[1], 2), own, number, TOK_DEV, N_DOM, 2, CAP, 2))(candidates_keys, candidates_turns).reshape((PARTS_SIZE, 2))
    defocus = touch_ends(jax.random.randint(key_of[2], (PARTS_SIZE,), 0, DEF), jax.random.fold_in(key_of[2], 1), 0, DEF - 1).astype(jnp.int32)
    ctf_table = draw_ctf_table(jax.random.fold_in(key_of[6], 71), 0)
    references = draw_references(jax.random.fold_in(key_of[6], 71), 0)
    rotations = draw_rotations(jax.random.fold_in(key_of[6], 71), 0)
    return {"particles": particles, "candidates": candidates, "defocus": defocus, "ctf_table": ctf_table, "references": references, "rotations": rotations}


highest = lax.Precision.HIGHEST


def slot_layout(candidates):
    entries = candidates.reshape(N_DOM, 2 * TOK_DEV).astype(jnp.int32)
    owner_ids = jnp.arange(N_DOM, dtype=jnp.int32)
    onehot_owner = (entries[:, :, None] == owner_ids[None, None, :]).astype(jnp.int32)
    entry_rank = jnp.cumsum(onehot_owner, axis=1) - onehot_owner
    slot_of = jnp.sum(entry_rank * onehot_owner, axis=2).astype(jnp.int32)
    return entries, slot_of


def reference(particles, candidates, defocus, ctf_table, references, rotations):
    entries, slot_of = slot_layout(candidates)
    source_ids = jnp.broadcast_to(jnp.arange(N_DOM, dtype=jnp.int32)[:, None], entries.shape)
    entry_ids = jnp.broadcast_to(jnp.arange(2 * TOK_DEV, dtype=jnp.int32)[None, :], entries.shape)
    slot_entry = jnp.full((N_DOM, N_DOM, CAP), -1, jnp.int32).at[entries, source_ids, slot_of].set(entry_ids)
    slot_total = N_DOM * CAP
    live_flat = (slot_entry >= 0).reshape(N_DOM, slot_total)
    src_rows = (jnp.arange(N_DOM, dtype=jnp.int32)[None, :, None] * TOK_DEV + jnp.maximum(slot_entry, 0) // 2).astype(jnp.int32).reshape(N_DOM, slot_total)
    turn_maps = rotations.astype(jnp.float32)
    ref_grid = references.astype(jnp.float32).reshape(CLASSES, CYCLES, ANG)
    rotated = jnp.einsum("cla,rba->crlb", ref_grid, turn_maps, precision=highest).astype(jnp.bfloat16)
    rotated = rotated.reshape(N_DOM, CPG * ROT, PIX)
    ctf_power = ctf_table * ctf_table
    inverse_noise = 4.0 / (PIX ** 0.5)
    kind_ids = jnp.arange(DEF, dtype=jnp.int32)

    def prepare(owner_rows, owner_live):
        defocus_rows = jnp.where(owner_live, defocus[owner_rows], -1)
        picked = (defocus_rows[:, None] == kind_ids[None, :]).astype(jnp.float32)
        ctf_rows = jnp.dot(picked, ctf_table, precision=highest)
        weighted = (particles[owner_rows].astype(jnp.float32) * ctf_rows).astype(jnp.bfloat16)
        return picked, weighted

    def score_group(packed):
        owner_rows, owner_live, owner_refs = packed
        picked, weighted = prepare(owner_rows, owner_live)
        cross_term = jnp.dot(weighted, owner_refs.T, preferred_element_type=jnp.float32)
        square = owner_refs.astype(jnp.float32) ** 2
        energy = jnp.dot(ctf_power, square.T, precision=highest)
        energy_rows = jnp.dot(picked, energy, precision=highest)
        return inverse_noise * (cross_term - 0.5 * energy_rows)

    scores = lax.map(score_group, (src_rows, live_flat, rotated))
    slot_max = jnp.max(scores, axis=2)
    slot_sum = jnp.sum(jnp.exp(scores - slot_max[:, :, None]), axis=2)
    flat_slot = jnp.arange(N_DOM, dtype=jnp.int32)[:, None] * CAP + slot_of
    pair_max = slot_max[entries, flat_slot].reshape(PARTS_SIZE, 2)
    pair_sum = slot_sum[entries, flat_slot].reshape(PARTS_SIZE, 2)
    pair_best = jnp.max(pair_max, axis=1, keepdims=True)
    log_evidence = pair_best[:, 0] + jnp.log(jnp.sum(pair_sum * jnp.exp(pair_max - pair_best), axis=1))

    def accumulate(packed):
        owner_rows, owner_live, owner_scores = packed
        picked, weighted = prepare(owner_rows, owner_live)
        weights = jnp.where(owner_live[:, None], jnp.exp(owner_scores - log_evidence[owner_rows][:, None]), 0.0).astype(jnp.bfloat16)
        rot_sum = jnp.dot(weights.T, weighted, preferred_element_type=jnp.float32)
        pair_kind = jnp.dot(weights.astype(jnp.float32).T, picked, precision=highest)
        rot_weight = jnp.dot(pair_kind, ctf_power, precision=highest)
        back_sum = jnp.einsum("crlb,rba->cla", rot_sum.reshape(CPG, ROT, CYCLES, ANG), turn_maps, precision=highest)
        back_weight = jnp.einsum("crlb,rba->cla", rot_weight.reshape(CPG, ROT, CYCLES, ANG), turn_maps, precision=highest)
        return back_sum.reshape(CPG, PIX).astype(jnp.bfloat16), back_weight.reshape(CPG, PIX)

    class_sums, class_weights = lax.map(accumulate, (src_rows, live_flat, scores))
    return class_sums.reshape(CLASSES, PIX), class_weights.reshape(CLASSES, PIX), log_evidence
```

```python
import functools

import jax
import jax.numpy as jnp
from jax import lax
from jax.experimental import pallas as pl
from jax.experimental.pallas import tpu as pltpu
from jax.sharding import PartitionSpec as P

F32 = jnp.float32
BF16 = jnp.bfloat16
I32 = jnp.int32
MESH = pl.DeviceIdType.MESH
NT = (((1,), (1,)), ((), ()))
NN = (((1,), (0,)), ((), ()))

GROUPS = 64
SLOTS = 64
ANG = 64
CYC = 16
CPG = 4
ROT = 64
PAIRS = CPG * ROT
PIX = CYC * ANG
KINDS = 32
TOK = 1024
SHARES = 4
ROWS = 640
PACKED = SHARES * ROWS
HI = ROWS // 64
VMEM_LIMIT = 60 * 1024 * 1024


def mm(a, b, dims=NN):
    return lax.dot_general(a, b, dims, preferred_element_type=F32)


def iota(shape, dim):
    return lax.broadcasted_iota(I32, shape, dim)


def pieces(x):
    p1 = x.astype(BF16)
    r1 = x - p1.astype(F32)
    p2 = r1.astype(BF16)
    p3 = (r1 - p2.astype(F32)).astype(BF16)
    return p1, p2, p3


def onehot(mask):
    return jnp.where(mask, 1.0, 0.0).astype(BF16)


def vm(n):
    return [pl.BlockSpec(memory_space=pltpu.VMEM)] * n


def route(cand_ref, kind_ref, tab_ref, kinds_ref, rho_ref):
    g_iota = iota((GROUPS, TOK), 0)
    tri = onehot(iota((256, 256), 0) < iota((256, 256), 1))
    count = jnp.zeros((GROUPS, 1), F32)
    owners, ranks = [], []
    for j in range(2):
        owner = onehot(g_iota == cand_ref[j : j + 1, :])
        owners.append(owner)
        row = []
        for blk in range(TOK // 256):
            part = owner[:, blk * 256 : (blk + 1) * 256]
            before = mm(part, tri) + count
            row.append(jnp.sum(before * part.astype(F32), axis=0, keepdims=True))
            count = count + jnp.sum(part.astype(F32), axis=1, keepdims=True)
        ranks.append(jnp.concatenate(row, axis=1))
    padded = jnp.floor((count + 7.0) * 0.125) * 8.0
    low = onehot(iota((GROUPS, GROUPS), 1) < iota((GROUPS, GROUPS), 0))
    offset = mm(low, jnp.broadcast_to(padded, (GROUPS, 128)).astype(BF16))[:, 0:1]
    tok = iota((1, TOK), 1)
    s_iota = iota((SLOTS, TOK), 0)
    high = jnp.zeros((GROUPS, SLOTS), F32)
    low_part = jnp.zeros((GROUPS, SLOTS), F32)
    for j in range(2):
        slot = onehot(s_iota == ranks[j].astype(I32))
        v1 = (tok // 8).astype(F32)
        v2 = ((tok % 8) * 32 + kind_ref[...]).astype(F32)
        high = high + mm(owners[j], (slot.astype(F32) * v1).astype(BF16), NT)
        low_part = low_part + mm(owners[j], (slot.astype(F32) * v2).astype(BF16), NT)
        at = jnp.sum(owners[j].astype(F32) * offset, axis=0, keepdims=True) + ranks[j]
        rho_ref[j : j + 1, :] = at.astype(I32)
    low_int = low_part.astype(I32)
    kinds = low_int % 32
    token = high.astype(I32) * 8 + low_int // 32
    s_lane = iota((GROUPS, SLOTS), 1)
    live = s_lane < count.astype(I32)
    tab_ref[:, 0:SLOTS] = token + 1024 * kinds
    extra = jnp.where(s_lane == 0, offset, jnp.where(s_lane == 1, count, padded))
    tab_ref[:, SLOTS : 2 * SLOTS] = extra.astype(I32)
    kinds_ref[:, 0:SLOTS] = jnp.where(live, kinds, -1)
    kinds_ref[:, SLOTS : 2 * SLOTS] = jnp.full((GROUPS, SLOTS), -1, I32)


def start_kernel(cand_ref, kind_ref, mine_ref, tab_ref, kinds_ref, rho_ref, all_ref, send_sem, recv_sem, own_sem):
    me = lax.axis_index("dom")
    row = lax.axis_index("cls")
    barrier = pltpu.get_barrier_semaphore()

    def greet(i, _):
        pl.semaphore_signal(barrier, inc=1, device_id=(row, lax.rem(me + i, GROUPS)), device_id_type=MESH)
        return 0

    lax.fori_loop(1, GROUPS, greet, 0)
    pl.semaphore_wait(barrier, GROUPS - 1)

    def copy(i):
        return pltpu.make_async_remote_copy(
            src_ref=mine_ref,
            dst_ref=all_ref.at[me],
            send_sem=send_sem.at[i],
            recv_sem=recv_sem.at[i],
            device_id=(row, lax.rem(me + i, GROUPS)),
            device_id_type=MESH,
        )

    def send(i, _):
        copy(i).start()
        return 0

    lax.fori_loop(1, GROUPS, send, 0)
    own = pltpu.make_async_copy(mine_ref, all_ref.at[me], own_sem)
    own.start()
    route(cand_ref, kind_ref, tab_ref, kinds_ref, rho_ref)
    own.wait()

    def finish(i, _):
        copy(i).wait()
        return 0

    lax.fori_loop(1, GROUPS, finish, 0)


def start_stage(cand_t, kinds_row, mine):
    return pl.pallas_call(
        start_kernel,
        out_shape=(
            jax.ShapeDtypeStruct((GROUPS, 2 * SLOTS), I32),
            jax.ShapeDtypeStruct((GROUPS, 2 * SLOTS), I32),
            jax.ShapeDtypeStruct((2, TOK), I32),
            jax.ShapeDtypeStruct((GROUPS, 32, 128), BF16),
        ),
        in_specs=vm(3),
        out_specs=tuple(vm(4)),
        scratch_shapes=[
            pltpu.SemaphoreType.DMA((GROUPS,)),
            pltpu.SemaphoreType.DMA((GROUPS,)),
            pltpu.SemaphoreType.DMA,
        ],
        compiler_params=pltpu.CompilerParams(collective_id=0, has_side_effects=True, vmem_limit_bytes=VMEM_LIMIT),
        name="start_stage",
    )(cand_t, kinds_row, mine)


def score_kernel(tab_ref, part_ref, refs_ref, rotq_ref, ctf_ref, kinds_ref, out_ref, wout_ref, xs, cs, spread, power, perm, stage, wext, rext):
    def make_perm(i, _):
        r = iota((64, PIX), 0) + i * 64
        c = iota((64, PIX), 1)
        hit = (c // CYC == r % ANG) & (c % CYC == r // ANG)
        perm[pl.ds(pl.multiple_of(i * 64, 64), 64), :] = onehot(hit)
        return 0

    lax.fori_loop(0, PIX // 64, make_perm, 0)

    def turn_rows(i, _):
        y = mm(part_ref[pl.ds(pl.multiple_of(i * 128, 128), 128), :], perm[...])
        for j in range(8):
            xs[pl.ds(i * 1024 + j, 128, stride=8), :] = y[:, j * 128 : (j + 1) * 128]
        return 0

    lax.fori_loop(0, TOK // 128, turn_rows, 0)
    for j in range(8):
        cs[pl.ds(j, KINDS, stride=8), :] = ctf_ref[:, j * 128 : (j + 1) * 128]
    square = ctf_ref[...] * ctf_ref[...]
    s1 = square.astype(BF16)
    s2 = (square - s1.astype(F32)).astype(BF16)
    for j in range(4):
        power[j * 32 : (j + 1) * 32, :] = s1 if j < 3 else jnp.zeros_like(s1)
        power[128 + j * 32 : 128 + (j + 1) * 32, :] = s2 if j < 3 else jnp.zeros_like(s2)
    ri = iota((128, 256), 0)
    ci = iota((128, 256), 1)
    want = (ci // 64) * CYC + ci % CYC
    rep = [onehot(ri == want + 64 * h) for h in range(2)]

    def spread_refs(g, _):
        flat = refs_ref[g]
        for h in range(2):
            spread[pl.ds(pl.multiple_of(g * 64 + h * 32, 32), 32), :] = mm(flat, rep[h]).astype(BF16)
        return 0

    lax.fori_loop(0, GROUPS, spread_refs, 0)
    out_ref[...] = jnp.zeros_like(out_ref)
    stage[...] = jnp.zeros_like(stage)
    lane = iota((1, 256), 1)
    masks = [onehot((lane // CYC) % 4 == b) for b in range(4)]
    half = iota((1, 128), 1) < 64
    lane_e = iota((1, 128), 1)
    k_row = iota((128, 128), 0)

    def group(g, _):
        base = spread[pl.ds(pl.multiple_of(g * 64, 64), 64), :]
        block = jnp.concatenate([base * m for m in masks], axis=0)
        for part in range(4):
            t = mm(rotq_ref[part * 256 : (part + 1) * 256, :], block)
            for pair in range(2):
                qp = part * 2 + pair
                for c in range(2):
                    a = t[pair * 128 : pair * 128 + 64, c * 128 : (c + 1) * 128]
                    b = t[pair * 128 + 64 : pair * 128 + 128, c * 128 : (c + 1) * 128]
                    e = jnp.where(half, a, pltpu.roll(b, 64, 1)).astype(BF16)
                    o = jnp.where(half, pltpu.roll(a, 64, 1), b).astype(BF16)
                    rext[c * 128 : c * 128 + 64, qp * 128 : (qp + 1) * 128] = e
                    rext[c * 128 + 64 : c * 128 + 128, qp * 128 : (qp + 1) * 128] = o
        rot = rext[:, 0:PIX]
        en = mm(rot * rot, power[...], NT)
        en = -0.5 * (en[:, 0:128] + en[:, 128:256])
        p1, p2, p3 = pieces(en)
        ext = jnp.where(lane_e < 32, p1.astype(F32), jnp.where(lane_e < 64, p2.astype(F32), jnp.where(lane_e < 96, p3.astype(F32), 0.0)))
        rext[:, PIX : PIX + 128] = ext.astype(BF16)
        def gather(i, _):
            for u in range(8):
                entry = tab_ref[g, i * 8 + u]
                p = entry % 1024
                k = entry // 1024
                x = xs[pl.ds(pl.multiple_of(p * 8, 8), 8), :]
                w = cs[pl.ds(pl.multiple_of(k * 8, 8), 8), :]
                stage[pl.ds(pl.multiple_of((i * 8 + u) * 8, 8), 8), :] = x * w
            return 0

        lax.fori_loop(0, tab_ref[g, SLOTS + 2] // 8, gather, 0)
        for j in range(8):
            col = stage[pl.ds(j, SLOTS, stride=8), :].astype(BF16)
            wext[:, j * 128 : (j + 1) * 128] = col
            wout_ref[g, :, j * 128 : (j + 1) * 128] = col
        kinds = kinds_ref[pl.ds(g, 1), :]
        hit = jnp.where(((k_row % 32) == kinds) & (k_row < 96), 1.0, 0.0)
        wext[:, PIX : PIX + 128] = jnp.transpose(hit)[0:SLOTS, :].astype(BF16)
        scores = mm(wext[...], rext[...], NT) * (4.0 / 64.0)
        out_ref[pl.ds(pl.multiple_of(tab_ref[g, SLOTS], 8), SLOTS), :] = scores
        return 0

    lax.fori_loop(0, GROUPS, group, 0)


def score_stage(tab, particles, refs, rotq, ctf, kinds):
    return pl.pallas_call(
        score_kernel,
        out_shape=(
            jax.ShapeDtypeStruct((PACKED, PAIRS), F32),
            jax.ShapeDtypeStruct((GROUPS, SLOTS, PIX), BF16),
        ),
        in_specs=[pl.BlockSpec(memory_space=pltpu.SMEM)] + vm(5),
        out_specs=tuple(vm(2)),
        scratch_shapes=[
            pltpu.VMEM((TOK * 8, 128), F32),
            pltpu.VMEM((KINDS * 8, 128), F32),
            pltpu.VMEM((GROUPS * 64, 256), BF16),
            pltpu.VMEM((256, PIX), BF16),
            pltpu.VMEM((PIX, PIX), BF16),
            pltpu.VMEM((SLOTS * 8, 128), F32),
            pltpu.VMEM((SLOTS, PIX + 128), BF16),
            pltpu.VMEM((PAIRS, PIX + 128), BF16),
        ],
        compiler_params=pltpu.CompilerParams(vmem_limit_bytes=VMEM_LIMIT),
        name="score_stage",
    )(tab, particles, refs, rotq, ctf, kinds)


def soft_kernel(part_ref, rho_ref, w_ref, log_ref, recv, stat, stat_recv, total, sems):
    me = lax.axis_index("cls")
    dom = lax.axis_index("dom")
    barrier = pltpu.get_barrier_semaphore()
    for d in range(1, SHARES):
        pl.semaphore_signal(barrier, inc=1, device_id=(lax.rem(me + d, SHARES), dom), device_id_type=MESH)
    pl.semaphore_wait(barrier, SHARES - 1)

    def copy(step, d, src, dst):
        return pltpu.make_async_remote_copy(
            src_ref=src,
            dst_ref=dst,
            send_sem=sems.at[step, 0, d],
            recv_sem=sems.at[step, 1, d],
            device_id=(lax.rem(me + d, SHARES), dom),
            device_id_type=MESH,
        )

    first = [copy(0, d, part_ref.at[lax.rem(me + d, SHARES)], recv.at[d - 1]) for d in (2, 1, 3)]
    for c in first:
        c.start()
    for c in first:
        c.wait()
    lanes = iota((64, 128), 1)
    top = jnp.zeros((64, 128), F32)
    tot = jnp.zeros((64, 128), F32)
    for j in range(HI):
        at = pl.ds(j * 64, 64)
        x = part_ref[me, at, :] + recv[0, at, :] + recv[1, at, :] + recv[2, at, :]
        total[at, :] = x
        m = jnp.max(x, axis=1, keepdims=True)
        s = jnp.sum(jnp.exp(x - m), axis=1, keepdims=True)
        here = lanes == me * HI + j
        top = jnp.where(here, m, top)
        tot = jnp.where(here, s, tot)
    stat[0] = top
    stat[1] = tot
    second = [copy(1, d, stat, stat_recv.at[d - 1]) for d in (2, 1, 3)]
    for c in second:
        c.start()
    for c in second:
        c.wait()
    top = stat[0] + stat_recv[0, 0] + stat_recv[1, 0] + stat_recv[2, 0]
    tot = stat[1] + stat_recv[0, 1] + stat_recv[1, 1] + stat_recv[2, 1]
    three = jnp.concatenate(list(pieces(top)) + list(pieces(tot)), axis=0)
    maxima, sums, his, los = [], [], [], []
    for j in range(2):
        rho = rho_ref[j : j + 1, :]
        hi = onehot(iota((128, TOK), 0) == rho // 64)
        lo = jnp.where(iota((64, TOK), 0) == rho % 64, 1.0, 0.0)
        t = mm(three, hi)
        maxima.append(jnp.sum((t[0:64] + t[64:128] + t[128:192]) * lo, axis=0, keepdims=True))
        sums.append(jnp.sum((t[192:256] + t[256:320] + t[320:384]) * lo, axis=0, keepdims=True))
        his.append(hi)
        los.append(lo)
    best = jnp.maximum(maxima[0], maxima[1])
    log = best + jnp.log(sums[0] * jnp.exp(maxima[0] - best) + sums[1] * jnp.exp(maxima[1] - best))
    log_ref[...] = log
    back = jnp.zeros((64, 128), F32)
    for j in range(2):
        for p in pieces(log):
            back = back + mm((los[j] * p.astype(F32)).astype(BF16), his[j], NT)
    for j in range(HI):
        at = pl.ds(j * 64, 64)
        col = jnp.sum(jnp.where(lanes == me * HI + j, back, 0.0), axis=1, keepdims=True)
        w_ref[me, at, :] = jnp.exp(total[at, :] - col).astype(BF16)
    third = [copy(2, d, w_ref.at[me], w_ref.at[me]) for d in (2, 1, 3)]
    for c in third:
        c.start()
    for c in third:
        c.wait()


def soft_stage(scores, rho):
    return pl.pallas_call(
        soft_kernel,
        out_shape=(
            jax.ShapeDtypeStruct((SHARES, ROWS, PAIRS), BF16),
            jax.ShapeDtypeStruct((1, TOK), F32),
        ),
        in_specs=vm(2),
        out_specs=tuple(vm(2)),
        scratch_shapes=[
            pltpu.VMEM((SHARES - 1, ROWS, PAIRS), F32),
            pltpu.VMEM((2, 64, 128), F32),
            pltpu.VMEM((SHARES - 1, 2, 64, 128), F32),
            pltpu.VMEM((ROWS, PAIRS), F32),
            pltpu.SemaphoreType.DMA((3, 2, SHARES)),
        ],
        compiler_params=pltpu.CompilerParams(collective_id=1, has_side_effects=True, vmem_limit_bytes=VMEM_LIMIT),
        name="soft_stage",
    )(scores.reshape(SHARES, ROWS, PAIRS), rho)


def turned_back(rows_of, rott_ref, rsq):
    half = iota((1, 128), 1) < 64
    for n in range(4):
        t = rows_of(n)
        for pair in range(2):
            qp = n * 2 + pair
            for c in range(2):
                a = t[c * 128 : c * 128 + 64, pair * 128 : (pair + 1) * 128]
                b = t[c * 128 + 64 : c * 128 + 128, pair * 128 : (pair + 1) * 128]
                e = jnp.where(half, a, pltpu.roll(b, 64, 1)).astype(BF16)
                o = jnp.where(half, pltpu.roll(a, 64, 1), b).astype(BF16)
                rsq[qp * 128 : qp * 128 + 64, c * 128 : (c + 1) * 128] = e
                rsq[qp * 128 + 64 : qp * 128 + 128, c * 128 : (c + 1) * 128] = o
    full = mm(rott_ref[...], rsq[...])
    lane = iota((1, 256), 1)
    diag = jnp.zeros((64, 256), F32)
    for b in range(4):
        diag = jnp.where((lane // CYC) % 4 == b, full[b * 64 : (b + 1) * 64, :], diag)
    ri = iota((256, 128), 0)
    ci = iota((256, 128), 1)
    want = (ri // 64) * CYC + ri % CYC
    p1 = diag.astype(BF16)
    p2 = (diag - p1.astype(F32)).astype(BF16)
    out = jnp.zeros((32, 128), F32)
    for h in range(2):
        fold = onehot(ci == want + 64 * h)
        out = out + mm(p1[h * 32 : (h + 1) * 32], fold) + mm(p2[h * 32 : (h + 1) * 32], fold)
    return out


def sum_kernel(tab_ref, w_ref, weighted_ref, rott_ref, kinds_ref, sums_ref, pk_ref, wide, rsq):
    me = lax.axis_index("cls")
    for i in range(SHARES):
        wide[i * ROWS : (i + 1) * ROWS, :] = w_ref[i].astype(F32)
    s_col = iota((SLOTS, PAIRS), 0)
    k_col = iota((8, 128), 0) + me * 8

    def group(g, _):
        at = pl.multiple_of(tab_ref[g, SLOTS], 8)
        w = wide[pl.ds(at, SLOTS), :]
        w = jnp.where(s_col < tab_ref[g, SLOTS + 1], w, 0.0)
        wt = jnp.transpose(w).astype(BF16)
        out = turned_back(lambda n: mm(wt, weighted_ref[g, :, n * 256 : (n + 1) * 256]), rott_ref, rsq)
        sums_ref[g] = out.astype(BF16)
        kinds = kinds_ref[pl.ds(g, 1), :]
        hit = onehot(k_col == kinds)[:, 0:SLOTS]
        pk_ref[g] = mm(hit, w.astype(BF16))
        return 0

    lax.fori_loop(0, GROUPS, group, 0)


def sum_stage(tab, w, weighted, rott, kinds):
    return pl.pallas_call(
        sum_kernel,
        out_shape=(
            jax.ShapeDtypeStruct((GROUPS, 32, 128), BF16),
            jax.ShapeDtypeStruct((GROUPS, 8, PAIRS), F32),
        ),
        in_specs=[pl.BlockSpec(memory_space=pltpu.SMEM)] + vm(4),
        out_specs=tuple(vm(2)),
        scratch_shapes=[
            pltpu.VMEM((PACKED, PAIRS), F32),
            pltpu.VMEM((1024, 256), BF16),
        ],
        compiler_params=pltpu.CompilerParams(vmem_limit_bytes=VMEM_LIMIT),
        name="sum_stage",
    )(tab, w, weighted, rott, kinds)


def end_kernel(sums_ref, pk_ref, ctf_ref, rott_ref, cs_ref, cw_ref, got, got_pk, mine, others, rsq, ssem, rsem, sems):
    me = lax.axis_index("dom")
    row = lax.axis_index("cls")
    barrier = pltpu.get_barrier_semaphore()

    def greet(i, _):
        pl.semaphore_signal(barrier, inc=1, device_id=(row, lax.rem(me + i, GROUPS)), device_id_type=MESH)
        return 0

    lax.fori_loop(1, GROUPS, greet, 0)
    for d in range(1, SHARES):
        pl.semaphore_signal(barrier, inc=1, device_id=(lax.rem(row + d, SHARES), me), device_id_type=MESH)
    pl.semaphore_wait(barrier, GROUPS - 1 + SHARES - 1)

    def copies(i):
        to = lax.rem(me + i, GROUPS)
        return [
            pltpu.make_async_remote_copy(
                src_ref=src.at[to],
                dst_ref=dst.at[i],
                send_sem=ssem.at[n, i],
                recv_sem=rsem.at[n, i],
                device_id=(row, to),
                device_id_type=MESH,
            )
            for n, (src, dst) in enumerate(((pk_ref, got_pk), (sums_ref, got)))
        ]

    def send(i, _):
        for c in copies(i):
            c.start()
        return 0

    lax.fori_loop(1, GROUPS, send, 0)

    def wait_pk(i, acc):
        copies(i)[0].wait()
        return acc + got_pk[i]

    acc = lax.fori_loop(1, GROUPS, wait_pk, pk_ref[me])
    mine[...] = acc

    def share(d):
        return pltpu.make_async_remote_copy(
            src_ref=mine,
            dst_ref=others.at[d - 1],
            send_sem=sems.at[0, d],
            recv_sem=sems.at[1, d],
            device_id=(lax.rem(row + d, SHARES), me),
            device_id_type=MESH,
        )

    for d in range(1, SHARES):
        share(d).start()

    def wait_sums(i, acc):
        copies(i)[1].wait()
        return acc + got[i].astype(F32)

    acc = lax.fori_loop(1, GROUPS, wait_sums, sums_ref[me].astype(F32))

    def placed(x, ref):
        t = jnp.transpose(x)
        ref[:, 0:32] = t[0:64, :].astype(ref.dtype)
        ref[:, 32:64] = t[64:128, :].astype(ref.dtype)

    placed(acc, cs_ref)
    for d in range(1, SHARES):
        share(d).wait()
    rows = []
    for k in range(SHARES):
        x = mine[...]
        for d in range(1, SHARES):
            x = jnp.where(lax.rem(k + d, SHARES) == row, others[d - 1], x)
        rows.append(x)
    pkt = jnp.transpose(jnp.concatenate(rows, axis=0))
    power = ctf_ref[...] * ctf_ref[...]

    def columns(n):
        return lax.dot_general(
            pkt, power[:, n * 256 : (n + 1) * 256], NN, precision=lax.Precision.HIGHEST, preferred_element_type=F32
        )

    placed(turned_back(columns, rott_ref, rsq), cw_ref)


def end_stage(sums, pk, ctf, rott):
    return pl.pallas_call(
        end_kernel,
        out_shape=(
            jax.ShapeDtypeStruct((64, 64), BF16),
            jax.ShapeDtypeStruct((64, 64), F32),
        ),
        in_specs=vm(4),
        out_specs=tuple(vm(2)),
        scratch_shapes=[
            pltpu.VMEM((GROUPS, 32, 128), BF16),
            pltpu.VMEM((GROUPS, 8, PAIRS), F32),
            pltpu.VMEM((8, PAIRS), F32),
            pltpu.VMEM((SHARES - 1, 8, PAIRS), F32),
            pltpu.VMEM((1024, 256), BF16),
            pltpu.SemaphoreType.DMA((2, GROUPS)),
            pltpu.SemaphoreType.DMA((2, GROUPS)),
            pltpu.SemaphoreType.DMA((2, SHARES)),
        ],
        compiler_params=pltpu.CompilerParams(collective_id=2, has_side_effects=True, vmem_limit_bytes=VMEM_LIMIT),
        name="end_stage",
    )(sums, pk, ctf, rott)


def prepared(candidates, defocus, ctf_table, references, rotations):
    mine = references.reshape(CPG, CYC, 2, 32).transpose(3, 2, 0, 1).reshape(32, 128)
    rotq = rotations.reshape(ROT, CYC, 4, ANG).transpose(1, 0, 2, 3).reshape(1024, 256)
    rott = rotq.T
    ctf = ctf_table.reshape(KINDS, CYC, ANG).transpose(0, 2, 1).reshape(KINDS, PIX)
    return mine, rotq, rott, ctf, candidates.T, defocus.reshape(1, TOK)


def local(particles, candidates, defocus, ctf_table, references, rotations):
    mine, rotq, rott, ctf, cand_t, kinds_row = prepared(candidates, defocus, ctf_table, references, rotations)
    tab, kinds, rho, refs = start_stage(cand_t, kinds_row, mine)
    scores, weighted = score_stage(tab, particles, refs, rotq, ctf, kinds)
    w, log = soft_stage(scores, rho)
    sums, pk = sum_stage(tab, w, weighted, rott, kinds)
    cs, cw = end_stage(sums, pk, ctf, rott)
    return cs.reshape(CPG, PIX), cw.reshape(CPG, PIX), log.reshape(TOK)


def solution(mesh):
    in_specs = (P("dom", "cls"), P("dom", None), P("dom"), P(None, "cls"), P("dom", "cls"), P())
    out_specs = (P("dom", "cls"), P("dom", "cls"), P("dom"))
    return jax.shard_map(local, mesh=mesh, in_specs=in_specs, out_specs=out_specs, check_vma=False)
```

```python
import functools

import jax
import jax.numpy as jnp
from jax import lax
from jax.experimental import pallas as pl
from jax.experimental.pallas import tpu as pltpu
from jax.sharding import PartitionSpec as P

F32 = jnp.float32
BF16 = jnp.bfloat16
I32 = jnp.int32
MESH = pl.DeviceIdType.MESH
NT = (((1,), (1,)), ((), ()))
NN = (((1,), (0,)), ((), ()))

GROUPS = 64
SLOTS = 64
ANG = 64
CYC = 16
CPG = 4
ROT = 64
PAIRS = CPG * ROT
PIX = CYC * ANG
KINDS = 32
TOK = 1024
SHARES = 4
ROWS = 640
PACKED = SHARES * ROWS
HI = ROWS // 64
VMEM_LIMIT = 60 * 1024 * 1024


def mm(a, b, dims=NN):
    return lax.dot_general(a, b, dims, preferred_element_type=F32)


def iota(shape, dim):
    return lax.broadcasted_iota(I32, shape, dim)


def pieces(x):
    p1 = x.astype(BF16)
    r1 = x - p1.astype(F32)
    p2 = r1.astype(BF16)
    p3 = (r1 - p2.astype(F32)).astype(BF16)
    return p1, p2, p3


def onehot(mask):
    return jnp.where(mask, 1.0, 0.0).astype(BF16)


def vm(n):
    return [pl.BlockSpec(memory_space=pltpu.VMEM)] * n


def route(cand_ref, kind_ref, tab_ref, kinds_ref, rho_ref):
    g_iota = iota((GROUPS, TOK), 0)
    tri = onehot(iota((256, 256), 0) < iota((256, 256), 1))
    count = jnp.zeros((GROUPS, 1), F32)
    owners, ranks = [], []
    for j in range(2):
        owner = onehot(g_iota == cand_ref[j : j + 1, :])
        owners.append(owner)
        row = []
        for blk in range(TOK // 256):
            part = owner[:, blk * 256 : (blk + 1) * 256]
            before = mm(part, tri) + count
            row.append(jnp.sum(before * part.astype(F32), axis=0, keepdims=True))
            count = count + jnp.sum(part.astype(F32), axis=1, keepdims=True)
        ranks.append(jnp.concatenate(row, axis=1))
    padded = jnp.floor((count + 7.0) * 0.125) * 8.0
    low = onehot(iota((GROUPS, GROUPS), 1) < iota((GROUPS, GROUPS), 0))
    offset = mm(low, jnp.broadcast_to(padded, (GROUPS, 128)).astype(BF16))[:, 0:1]
    tok = iota((1, TOK), 1)
    s_iota = iota((SLOTS, TOK), 0)
    high = jnp.zeros((GROUPS, SLOTS), F32)
    low_part = jnp.zeros((GROUPS, SLOTS), F32)
    for j in range(2):
        slot = onehot(s_iota == ranks[j].astype(I32))
        v1 = (tok // 8).astype(F32)
        v2 = ((tok % 8) * 32 + kind_ref[...]).astype(F32)
        high = high + mm(owners[j], (slot.astype(F32) * v1).astype(BF16), NT)
        low_part = low_part + mm(owners[j], (slot.astype(F32) * v2).astype(BF16), NT)
        at = jnp.sum(owners[j].astype(F32) * offset, axis=0, keepdims=True) + ranks[j]
        rho_ref[j : j + 1, :] = at.astype(I32)
    low_int = low_part.astype(I32)
    kinds = low_int % 32
    token = high.astype(I32) * 8 + low_int // 32
    s_lane = iota((GROUPS, SLOTS), 1)
    live = s_lane < count.astype(I32)
    tab_ref[:, 0:SLOTS] = token * 8 + 65536 * 8 * kinds
    extra = jnp.where(s_lane == 0, offset, jnp.where(s_lane == 1, count, padded))
    tab_ref[:, SLOTS : 2 * SLOTS] = extra.astype(I32)
    kinds_ref[:, 0:SLOTS] = jnp.where(live, kinds, -1)
    kinds_ref[:, SLOTS : 2 * SLOTS] = jnp.full((GROUPS, SLOTS), -1, I32)


def turn_pixels(part_ref, xs_ref, perm):
    def make_perm(i, _):
        r = iota((64, PIX), 0)
        c = iota((64, PIX), 1)
        hit = c == (r * CYC + i)
        perm[pl.ds(pl.multiple_of(i * 64, 64), 64), :] = onehot(hit)
        return 0

    lax.fori_loop(0, CYC, make_perm, 0)

    def turn_rows(i, _):
        y = mm(part_ref[pl.ds(pl.multiple_of(i * 128, 128), 128), :], perm[...])
        for j in range(8):
            xs_ref[pl.ds(i * 1024 + j, 128, stride=8), :] = y[:, j * 128 : (j + 1) * 128]
        return 0

    lax.fori_loop(0, TOK // 128, turn_rows, 0)


def start_kernel(cand_ref, kind_ref, mine_ref, part_ref, tab_ref, kinds_ref, rho_ref, all_ref, xs_ref, perm, send_sem, recv_sem, own_sem):
    me = lax.axis_index("dom")
    row = lax.axis_index("cls")
    barrier = pltpu.get_barrier_semaphore()

    def greet(i, _):
        pl.semaphore_signal(barrier, inc=1, device_id=(row, lax.rem(me + i, GROUPS)), device_id_type=MESH)
        return 0

    lax.fori_loop(1, GROUPS, greet, 0)
    pl.semaphore_wait(barrier, GROUPS - 1)

    def copy(i):
        return pltpu.make_async_remote_copy(
            src_ref=mine_ref,
            dst_ref=all_ref.at[me],
            send_sem=send_sem.at[i],
            recv_sem=recv_sem.at[i],
            device_id=(row, lax.rem(me + i, GROUPS)),
            device_id_type=MESH,
        )

    def send(i, _):
        copy(i).start()
        return 0

    lax.fori_loop(1, GROUPS, send, 0)
    own = pltpu.make_async_copy(mine_ref, all_ref.at[me], own_sem)
    own.start()
    route(cand_ref, kind_ref, tab_ref, kinds_ref, rho_ref)
    turn_pixels(part_ref, xs_ref, perm)
    own.wait()

    def finish(i, _):
        copy(i).wait()
        return 0

    lax.fori_loop(1, GROUPS, finish, 0)


def start_stage(cand_t, kinds_row, mine, particles):
    return pl.pallas_call(
        start_kernel,
        out_shape=(
            jax.ShapeDtypeStruct((GROUPS, 2 * SLOTS), I32),
            jax.ShapeDtypeStruct((GROUPS, 2 * SLOTS), I32),
            jax.ShapeDtypeStruct((2, TOK), I32),
            jax.ShapeDtypeStruct((GROUPS, 32, 128), BF16),
            jax.ShapeDtypeStruct((TOK * 8, 128), F32),
        ),
        in_specs=vm(4),
        out_specs=tuple(vm(5)),
        scratch_shapes=[
            pltpu.VMEM((PIX, PIX), BF16),
            pltpu.SemaphoreType.DMA((GROUPS,)),
            pltpu.SemaphoreType.DMA((GROUPS,)),
            pltpu.SemaphoreType.DMA,
        ],
        compiler_params=pltpu.CompilerParams(collective_id=0, has_side_effects=True, vmem_limit_bytes=VMEM_LIMIT),
        name="start_stage",
    )(cand_t, kinds_row, mine, particles)


def score_kernel(tab_ref, xs, refs_ref, rott_ref, ctf_ref, kinds_ref, out_ref, wout_ref, cs, power, bd, raw, rot_a, rot_b, stage_a, stage_b, weights_a, weights_b, hits_a, hits_b):
    rots, stages, weights, hits = (rot_a, rot_b), (stage_a, stage_b), (weights_a, weights_b), (hits_a, hits_b)
    for j in range(8):
        cs[pl.ds(j, KINDS, stride=8), :] = ctf_ref[:, j * 128 : (j + 1) * 128]
    square = -0.5 * (ctf_ref[...] * ctf_ref[...])
    s1 = square.astype(BF16)
    power[0:32, :] = s1
    power[32:64, :] = (square - s1.astype(F32)).astype(BF16)
    out_ref[...] = jnp.zeros_like(out_ref)
    bd[...] = jnp.zeros_like(bd)
    half = iota((1, 128), 1) < 64
    keep = jnp.broadcast_to(half, (64, 128))
    keep_16 = jnp.broadcast_to(half, (16, 128))
    blank = jnp.zeros((16, 128), BF16)
    k_row = iota((128, 128), 0)

    def rotate(pair):
        for u in range(2):
            for cl in range(2):
                x = refs_ref[pair * 2 + u, cl * 16 : (cl + 1) * 16, :]
                y = pltpu.roll(x, 64, 1)
                for ch, (low, high) in enumerate(((x, y), (y, x))):
                    at = u * 256 + (ch * 2 + cl) * 64
                    low = jnp.where(keep_16, low, blank)
                    high = jnp.where(keep_16, blank, high)
                    bd[at : at + 16, 0:128] = low
                    bd[at + 16 : at + 32, 0:128] = high
                    bd[at + 32 : at + 48, 128:256] = low
                    bd[at + 48 : at + 64, 128:256] = high
        for n in range(4):
            at = slice(n * 256, (n + 1) * 256)
            raw[:, at] = mm(bd[...], rott_ref[:, at]).astype(BF16)

    def arrange(pair, u):
        g = pair * 2 + u
        rot, stage, weighted = rots[u], stages[u], weights[u]
        for s in range(SLOTS):
            entry = tab_ref[g, s]
            p = entry & 65535
            k = lax.shift_right_logical(entry, 16)
            x = xs[pl.ds(pl.multiple_of(p, 8), 8), :]
            w = cs[pl.ds(pl.multiple_of(k, 8), 8), :]
            stage[s * 8 : (s + 1) * 8, :] = x * w
        for qp in range(8):
            for k in range(2):
                r0 = u * 256 + k * 128
                a = raw[r0 : r0 + 64, qp * 128 : (qp + 1) * 128]
                b = raw[r0 + 64 : r0 + 128, qp * 128 : (qp + 1) * 128]
                rot[qp * 128 : qp * 128 + 64, k * 128 : (k + 1) * 128] = jnp.where(keep, a, pltpu.roll(b, 64, 1))
                rot[qp * 128 + 64 : qp * 128 + 128, k * 128 : (k + 1) * 128] = jnp.where(keep, pltpu.roll(a, 64, 1), b)
        for j in range(8):
            col = stage[pl.ds(j, SLOTS, stride=8), :].astype(BF16)
            weighted[:, j * 128 : (j + 1) * 128] = col
            wout_ref[g, :, j * 128 : (j + 1) * 128] = col
        kinds = kinds_ref[pl.ds(g, 1), :]
        hit = jnp.where(((k_row & 31) == kinds) & (k_row < 64), 1.0, 0.0)
        hits[u][...] = jnp.transpose(hit)[0:SLOTS, :].astype(BF16)

    def score(pair, u):
        g = pair * 2 + u
        rot, weighted = rots[u], weights[u]
        en, total = None, None
        for part in range(2):
            at = slice(part * 512, (part + 1) * 512)
            r = rot[at, :]
            z = mm(weighted[:, at], r)
            y = mm(power[:, at], r * r)
            total = z if total is None else total + z
            en = y if en is None else en + y
        en = en[0:32, :] + en[32:64, :]
        p1 = en.astype(BF16)
        p2 = (en - p1.astype(F32)).astype(BF16)
        total = total + mm(hits[u][:, 0:64], jnp.concatenate([p1, p2], axis=0))
        out_ref[pl.ds(pl.multiple_of(tab_ref[g, SLOTS], 8), SLOTS), :] = total * (4.0 / 64.0)

    def step(t, _):
        for u in range(2):
            score(jnp.clip(t - 2, 0, GROUPS // 2 - 1), u)
        for u in range(2):
            arrange(jnp.clip(t - 1, 0, GROUPS // 2 - 1), u)
        rotate(jnp.minimum(t, GROUPS // 2 - 1))
        return 0

    lax.fori_loop(0, GROUPS // 2 + 2, step, 0)


def score_stage(tab, xs, refs, rott, ctf, kinds):
    return pl.pallas_call(
        score_kernel,
        out_shape=(
            jax.ShapeDtypeStruct((PACKED, PAIRS), F32),
            jax.ShapeDtypeStruct((GROUPS, SLOTS, PIX), BF16),
        ),
        in_specs=[pl.BlockSpec(memory_space=pltpu.SMEM)] + vm(5),
        out_specs=tuple(vm(2)),
        scratch_shapes=[
            pltpu.VMEM((KINDS * 8, 128), F32),
            pltpu.VMEM((64, PIX), BF16),
            pltpu.VMEM((512, 256), BF16),
            pltpu.VMEM((512, PIX), BF16),
            pltpu.VMEM((PIX, PAIRS), BF16),
            pltpu.VMEM((PIX, PAIRS), BF16),
            pltpu.VMEM((SLOTS * 8, 128), F32),
            pltpu.VMEM((SLOTS * 8, 128), F32),
            pltpu.VMEM((SLOTS, PIX), BF16),
            pltpu.VMEM((SLOTS, PIX), BF16),
            pltpu.VMEM((SLOTS, 128), BF16),
            pltpu.VMEM((SLOTS, 128), BF16),
        ],
        compiler_params=pltpu.CompilerParams(vmem_limit_bytes=VMEM_LIMIT),
        name="score_stage",
    )(tab, xs, refs, rott, ctf, kinds)


def soft_kernel(part_ref, rho_ref, w_ref, log_ref, far, held, near, stat, stat_recv, total, sems, ring):
    me = lax.axis_index("cls")
    dom = lax.axis_index("dom")
    barrier = pltpu.get_barrier_semaphore()
    for d in range(1, SHARES):
        pl.semaphore_signal(barrier, inc=1, device_id=(lax.rem(me + d, SHARES), dom), device_id_type=MESH)
    pl.semaphore_wait(barrier, SHARES - 1)

    def copy(step, d, src, dst):
        return pltpu.make_async_remote_copy(
            src_ref=src,
            dst_ref=dst,
            send_sem=sems.at[step, 0, d],
            recv_sem=sems.at[step, 1, d],
            device_id=(lax.rem(me + d, SHARES), dom),
            device_id_type=MESH,
        )

    right, left, across = lax.rem(me + 1, SHARES), lax.rem(me + 3, SHARES), lax.rem(me + 2, SHARES)
    low, high = pl.ds(0, ROWS // 2), pl.ds(ROWS // 2, ROWS // 2)

    def hop(n, to, src, dst):
        return pltpu.make_async_remote_copy(
            src_ref=src,
            dst_ref=dst,
            send_sem=ring.at[0, n],
            recv_sem=ring.at[1, n],
            device_id=(to, dom),
            device_id_type=MESH,
        )

    out_low = hop(0, right, part_ref.at[across, low], far.at[0])
    out_high = hop(1, left, part_ref.at[across, high], far.at[1])
    to_right = hop(2, right, part_ref.at[right, high], near.at[0, high])
    to_left = hop(3, left, part_ref.at[left, low], near.at[1, low])
    for c in (out_low, out_high, to_right, to_left):
        c.start()
    out_low.wait()
    held[0] = part_ref[right, low, :] + far[0]
    sum_right = hop(4, right, held.at[0], near.at[0, low])
    sum_right.start()
    out_high.wait()
    held[1] = part_ref[left, high, :] + far[1]
    sum_left = hop(5, left, held.at[1], near.at[1, high])
    sum_left.start()
    for c in (to_right, to_left, sum_right, sum_left):
        c.wait()
    lanes = iota((64, 128), 1)
    top = jnp.zeros((64, 128), F32)
    tot = jnp.zeros((64, 128), F32)
    for j in range(HI):
        at = pl.ds(j * 64, 64)
        x = part_ref[me, at, :] + near[0, at, :] + near[1, at, :]
        total[at, :] = x
        m = jnp.max(x, axis=1, keepdims=True)
        s = jnp.sum(jnp.exp(x - m), axis=1, keepdims=True)
        here = lanes == me * HI + j
        top = jnp.where(here, m, top)
        tot = jnp.where(here, s, tot)
    stat[0] = top
    stat[1] = tot
    second = [copy(1, d, stat, stat_recv.at[d - 1]) for d in (2, 1, 3)]
    for c in second:
        c.start()
    for c in second:
        c.wait()
    top = stat[0] + stat_recv[0, 0] + stat_recv[1, 0] + stat_recv[2, 0]
    tot = stat[1] + stat_recv[0, 1] + stat_recv[1, 1] + stat_recv[2, 1]
    three = jnp.concatenate(list(pieces(top)) + list(pieces(tot)), axis=0)
    maxima, sums, his, los = [], [], [], []
    for j in range(2):
        rho = rho_ref[j : j + 1, :]
        hi = onehot(iota((128, TOK), 0) == rho // 64)
        lo = jnp.where(iota((64, TOK), 0) == rho % 64, 1.0, 0.0)
        t = mm(three, hi)
        maxima.append(jnp.sum((t[0:64] + t[64:128] + t[128:192]) * lo, axis=0, keepdims=True))
        sums.append(jnp.sum((t[192:256] + t[256:320] + t[320:384]) * lo, axis=0, keepdims=True))
        his.append(hi)
        los.append(lo)
    best = jnp.maximum(maxima[0], maxima[1])
    log = best + jnp.log(sums[0] * jnp.exp(maxima[0] - best) + sums[1] * jnp.exp(maxima[1] - best))
    log_ref[...] = log
    back = jnp.zeros((64, 128), F32)
    for j in range(2):
        for p in pieces(log):
            back = back + mm((los[j] * p.astype(F32)).astype(BF16), his[j], NT)
    for j in range(HI):
        at = pl.ds(j * 64, 64)
        col = jnp.sum(jnp.where(lanes == me * HI + j, back, 0.0), axis=1, keepdims=True)
        w_ref[me, at, :] = jnp.exp(total[at, :] - col).astype(BF16)
    own_right = hop(6, right, w_ref.at[me], w_ref.at[me])
    own_left = hop(7, left, w_ref.at[me], w_ref.at[me])
    own_right.start()
    own_left.start()
    own_right.wait()
    on_right = hop(8, right, w_ref.at[left, low], w_ref.at[left, low])
    on_right.start()
    own_left.wait()
    on_left = hop(9, left, w_ref.at[right, high], w_ref.at[right, high])
    on_left.start()
    on_right.wait()
    on_left.wait()


def soft_stage(scores, rho):
    return pl.pallas_call(
        soft_kernel,
        out_shape=(
            jax.ShapeDtypeStruct((SHARES, ROWS, PAIRS), BF16),
            jax.ShapeDtypeStruct((1, TOK), F32),
        ),
        in_specs=vm(2),
        out_specs=tuple(vm(2)),
        scratch_shapes=[
            pltpu.VMEM((2, ROWS // 2, PAIRS), F32),
            pltpu.VMEM((2, ROWS // 2, PAIRS), F32),
            pltpu.VMEM((2, ROWS, PAIRS), F32),
            pltpu.VMEM((2, 64, 128), F32),
            pltpu.VMEM((SHARES - 1, 2, 64, 128), F32),
            pltpu.VMEM((ROWS, PAIRS), F32),
            pltpu.SemaphoreType.DMA((2, 2, SHARES)),
            pltpu.SemaphoreType.DMA((2, 10)),
        ],
        compiler_params=pltpu.CompilerParams(collective_id=1, has_side_effects=True, vmem_limit_bytes=VMEM_LIMIT),
        name="soft_stage",
    )(scores.reshape(SHARES, ROWS, PAIRS), rho)


def turned(raw, rsq):
    keep = jnp.broadcast_to(iota((1, 128), 1) < 64, (64, 128))
    for qp in range(8):
        for c in range(2):
            a = raw[c * 128 : c * 128 + 64, qp * 128 : (qp + 1) * 128]
            b = raw[c * 128 + 64 : c * 128 + 128, qp * 128 : (qp + 1) * 128]
            e = jnp.where(keep, a, pltpu.roll(b, 64, 1))
            o = jnp.where(keep, pltpu.roll(a, 64, 1), b)
            rsq[qp * 128 : qp * 128 + 64, c * 128 : (c + 1) * 128] = e
            rsq[qp * 128 + 64 : qp * 128 + 128, c * 128 : (c + 1) * 128] = o


def diagonal(rott_ref, rsq):
    lane = iota((1, 256), 1)
    total = None
    for part in range(2):
        at = slice(part * 512, (part + 1) * 512)
        full = mm(rott_ref[:, at], rsq[at, :])
        diag = full[0:64, :]
        for b in range(1, 4):
            diag = jnp.where((lane // CYC) % 4 == b, full[b * 64 : (b + 1) * 64, :], diag)
        total = diag if total is None else total + diag
    return total


def folds():
    ri = iota((256, 128), 0)
    ci = iota((256, 128), 1)
    want = (ri // 64) * CYC + ri % CYC
    return [onehot(ci == want + 64 * h) for h in range(2)]


def folded(parts, fold):
    out = None
    for x, f in zip(parts, fold):
        p1 = x.astype(BF16)
        p2 = (x - p1.astype(F32)).astype(BF16)
        y = mm(p1, f) + mm(p2, f)
        out = y if out is None else out + y
    return out


def sum_kernel(tab_ref, w_ref, weighted_ref, rott_ref, kinds_ref, sums_ref, pk_ref, wide, rsq_a, rsq_b, raw_a, raw_b, parts):
    rsqs, raws = (rsq_a, rsq_b), (raw_a, raw_b)
    me = lax.axis_index("cls")
    for i in range(SHARES):
        wide[i * ROWS : (i + 1) * ROWS, :] = w_ref[i].astype(F32)
    s_col = iota((SLOTS, PAIRS), 0)
    k_col = iota((8, 128), 0) + me * 8

    def spread_out(g, raw):
        at = pl.multiple_of(tab_ref[g, SLOTS], 8)
        w = wide[pl.ds(at, SLOTS), :]
        w = jnp.where(s_col < tab_ref[g, SLOTS + 1], w, 0.0)
        wt = jnp.transpose(w).astype(BF16)
        for n in range(4):
            at = slice(n * 256, (n + 1) * 256)
            raw[:, at] = mm(wt, weighted_ref[g, :, at]).astype(BF16)
        kinds = kinds_ref[pl.ds(g, 1), :]
        hit = onehot(k_col == kinds)[:, 0:SLOTS]
        pk_ref[g] = mm(hit, w.astype(BF16))

    def finish(g, rsq):
        diag = diagonal(rott_ref, rsq)
        for h in range(2):
            parts[h, pl.ds(pl.multiple_of(g * 32, 32), 32), :] = diag[h * 32 : (h + 1) * 32, :]

    def two(i, _):
        for odd in range(2):
            t = i * 2 + odd
            now, other = odd, 1 - odd
            last = jnp.clip(t - 2, 0, GROUPS - 1)
            new = jnp.minimum(t, GROUPS - 1)
            finish(last, rsqs[now])
            turned(raws[other], rsqs[other])
            spread_out(new, raws[now])
        return 0

    lax.fori_loop(0, GROUPS // 2 + 1, two, 0)
    fold = folds()

    def fold_eight(i, _):
        at = pl.ds(pl.multiple_of(i * 256, 256), 256)
        out = folded([parts[h, at, :] for h in range(2)], fold).astype(BF16)
        for j in range(8):
            sums_ref[i * 8 + j] = out[j * 32 : (j + 1) * 32, :]
        return 0

    lax.fori_loop(0, GROUPS // 8, fold_eight, 0)


def sum_stage(tab, w, weighted, rott, kinds):
    return pl.pallas_call(
        sum_kernel,
        out_shape=(
            jax.ShapeDtypeStruct((GROUPS, 32, 128), BF16),
            jax.ShapeDtypeStruct((GROUPS, 8, PAIRS), F32),
        ),
        in_specs=[pl.BlockSpec(memory_space=pltpu.SMEM)] + vm(4),
        out_specs=tuple(vm(2)),
        scratch_shapes=[
            pltpu.VMEM((PACKED, PAIRS), F32),
            pltpu.VMEM((1024, 256), BF16),
            pltpu.VMEM((1024, 256), BF16),
            pltpu.VMEM((PAIRS, PIX), BF16),
            pltpu.VMEM((PAIRS, PIX), BF16),
            pltpu.VMEM((2, GROUPS * 32, 256), F32),
        ],
        compiler_params=pltpu.CompilerParams(vmem_limit_bytes=VMEM_LIMIT),
        name="sum_stage",
    )(tab, w, weighted, rott, kinds)


def end_kernel(sums_ref, pk_ref, ctf_ref, rott_ref, cs_ref, cw_ref, got, got_pk, mine, others, rsq, raw, ssem, rsem, sems):
    me = lax.axis_index("dom")
    row = lax.axis_index("cls")
    barrier = pltpu.get_barrier_semaphore()

    def greet(i, _):
        pl.semaphore_signal(barrier, inc=1, device_id=(row, lax.rem(me + i, GROUPS)), device_id_type=MESH)
        return 0

    lax.fori_loop(1, GROUPS, greet, 0)
    for d in range(1, SHARES):
        pl.semaphore_signal(barrier, inc=1, device_id=(lax.rem(row + d, SHARES), me), device_id_type=MESH)
    pl.semaphore_wait(barrier, GROUPS - 1 + SHARES - 1)

    def copies(i):
        to = lax.rem(me + i, GROUPS)
        return [
            pltpu.make_async_remote_copy(
                src_ref=src.at[to],
                dst_ref=dst.at[i],
                send_sem=ssem.at[n, i],
                recv_sem=rsem.at[n, i],
                device_id=(row, to),
                device_id_type=MESH,
            )
            for n, (src, dst) in enumerate(((pk_ref, got_pk), (sums_ref, got)))
        ]

    def send(i, _):
        for c in copies(i):
            c.start()
        return 0

    lax.fori_loop(1, GROUPS, send, 0)

    def wait_pk(i, acc):
        copies(i)[0].wait()
        return acc + got_pk[i]

    acc = lax.fori_loop(1, GROUPS, wait_pk, pk_ref[me])
    mine[...] = acc

    def share(d):
        return pltpu.make_async_remote_copy(
            src_ref=mine,
            dst_ref=others.at[d - 1],
            send_sem=sems.at[0, d],
            recv_sem=sems.at[1, d],
            device_id=(lax.rem(row + d, SHARES), me),
            device_id_type=MESH,
        )

    for d in range(1, SHARES):
        share(d).start()

    def wait_sums(i, acc):
        copies(i)[1].wait()
        return acc + got[i].astype(F32)

    acc = lax.fori_loop(1, GROUPS, wait_sums, sums_ref[me].astype(F32))

    def placed(x, ref):
        t = jnp.transpose(x)
        ref[:, 0:32] = t[0:64, :].astype(ref.dtype)
        ref[:, 32:64] = t[64:128, :].astype(ref.dtype)

    placed(acc, cs_ref)
    for d in range(1, SHARES):
        share(d).wait()
    rows = []
    for k in range(SHARES):
        x = mine[...]
        for d in range(1, SHARES):
            x = jnp.where(lax.rem(k + d, SHARES) == row, others[d - 1], x)
        rows.append(x)
    pkt = jnp.transpose(jnp.concatenate(rows, axis=0))
    power = ctf_ref[...] * ctf_ref[...]

    for n in range(4):
        at = slice(n * 256, (n + 1) * 256)
        raw[:, at] = lax.dot_general(
            pkt, power[:, at], NN, precision=lax.Precision.HIGHEST, preferred_element_type=F32
        ).astype(BF16)
    turned(raw, rsq)
    diag = diagonal(rott_ref, rsq)
    placed(folded([diag[0:32], diag[32:64]], folds()), cw_ref)


def end_stage(sums, pk, ctf, rott):
    return pl.pallas_call(
        end_kernel,
        out_shape=(
            jax.ShapeDtypeStruct((64, 64), BF16),
            jax.ShapeDtypeStruct((64, 64), F32),
        ),
        in_specs=vm(4),
        out_specs=tuple(vm(2)),
        scratch_shapes=[
            pltpu.VMEM((GROUPS, 32, 128), BF16),
            pltpu.VMEM((GROUPS, 8, PAIRS), F32),
            pltpu.VMEM((8, PAIRS), F32),
            pltpu.VMEM((SHARES - 1, 8, PAIRS), F32),
            pltpu.VMEM((1024, 256), BF16),
            pltpu.VMEM((PAIRS, PIX), BF16),
            pltpu.SemaphoreType.DMA((2, GROUPS)),
            pltpu.SemaphoreType.DMA((2, GROUPS)),
            pltpu.SemaphoreType.DMA((2, SHARES)),
        ],
        compiler_params=pltpu.CompilerParams(collective_id=2, has_side_effects=True, vmem_limit_bytes=VMEM_LIMIT),
        name="end_stage",
    )(sums, pk, ctf, rott)


def prepared(candidates, defocus, ctf_table, references, rotations):
    mine = references.reshape(2, 2, CYC, ANG).transpose(1, 2, 0, 3).reshape(32, 128)
    rott = rotations.reshape(ROT, CYC, 4 * ANG).transpose(2, 1, 0).reshape(256, 1024)
    ctf = ctf_table.reshape(KINDS, CYC, ANG).transpose(0, 2, 1).reshape(KINDS, PIX)
    return mine, rott, ctf, candidates.T, defocus.reshape(1, TOK)


def local(particles, candidates, defocus, ctf_table, references, rotations):
    mine, rott, ctf, cand_t, kinds_row = prepared(candidates, defocus, ctf_table, references, rotations)
    tab, kinds, rho, refs, xs = start_stage(cand_t, kinds_row, mine, particles)
    scores, weighted = score_stage(tab, xs, refs, rott, ctf, kinds)
    w, log = soft_stage(scores, rho)
    sums, pk = sum_stage(tab, w, weighted, rott, kinds)
    cs, cw = end_stage(sums, pk, ctf, rott)
    return cs.reshape(CPG, PIX), cw.reshape(CPG, PIX), log.reshape(TOK)


def solution(mesh):
    in_specs = (P("dom", "cls"), P("dom", None), P("dom"), P(None, "cls"), P("dom", "cls"), P())
    out_specs = (P("dom", "cls"), P("dom", "cls"), P("dom"))
    return jax.shard_map(local, mesh=mesh, in_specs=in_specs, out_specs=out_specs, check_vma=False)
```

```python
import functools

import jax
import jax.numpy as jnp
from jax import lax
from jax.experimental import pallas as pl
from jax.experimental.pallas import tpu as pltpu
from jax.sharding import PartitionSpec as P

F32 = jnp.float32
BF16 = jnp.bfloat16
I32 = jnp.int32
MESH = pl.DeviceIdType.MESH
NT = (((1,), (1,)), ((), ()))
NN = (((1,), (0,)), ((), ()))

GROUPS = 64
SLOTS = 64
ANG = 64
CYC = 16
CPG = 4
ROT = 64
PAIRS = CPG * ROT
PIX = CYC * ANG
KINDS = 32
TOK = 1024
SHARES = 4
ROWS = 640
PACKED = SHARES * ROWS
CHUNKS = ROWS // 64
PAIRS_OF = GROUPS // 2
Z, X = 8, 4
VMEM_LIMIT = 60 * 1024 * 1024


def mm(a, b, dims=NN):
    return lax.dot_general(a, b, dims, preferred_element_type=F32)


def iota(shape, dim):
    return lax.broadcasted_iota(I32, shape, dim)


def pieces(x):
    p1 = x.astype(BF16)
    r1 = x - p1.astype(F32)
    p2 = r1.astype(BF16)
    p3 = (r1 - p2.astype(F32)).astype(BF16)
    return p1, p2, p3


def onehot(mask):
    return jnp.where(mask, 1.0, 0.0).astype(BF16)


def vm(n):
    return [pl.BlockSpec(memory_space=pltpu.VMEM)] * n


def route(me, cand_ref, kind_ref, tab_ref, kinds_ref, rho_ref, pack_ref):
    g_iota = iota((GROUPS, TOK), 0)
    tri = onehot(iota((256, 256), 0) < iota((256, 256), 1))
    count = jnp.zeros((GROUPS, 1), F32)
    owners, ranks = [], []
    for j in range(2):
        owner = onehot(g_iota == ((cand_ref[j : j + 1, :] - me) & (GROUPS - 1)))
        owners.append(owner)
        row = []
        for blk in range(TOK // 256):
            part = owner[:, blk * 256 : (blk + 1) * 256]
            before = mm(part, tri) + count
            row.append(jnp.sum(before * part.astype(F32), axis=0, keepdims=True))
            count = count + jnp.sum(part.astype(F32), axis=1, keepdims=True)
        ranks.append(jnp.concatenate(row, axis=1))
    padded = jnp.floor((count + 7.0) * 0.125) * 8.0
    low = onehot(iota((GROUPS, GROUPS), 1) < iota((GROUPS, GROUPS), 0))
    offset = mm(low, jnp.broadcast_to(padded, (GROUPS, 128)).astype(BF16))[:, 0:1]
    at = iota((GROUPS, 384), 1) * 8
    ended = jnp.where(at >= (offset + padded).astype(I32), 1, 0)
    where_in = jnp.sum(ended, axis=0, keepdims=True)
    first = jnp.sum(jnp.where(iota((GROUPS, 384), 0) == where_in, offset.astype(I32), 0), axis=0, keepdims=True)
    source = where_in * 8 + (iota((1, 384), 1) - lax.shift_right_logical(first, 3))
    pack_ref[...] = jnp.where(where_in < GROUPS, source, 0)
    tok = iota((1, TOK), 1)
    s_iota = iota((SLOTS, TOK), 0)
    high = jnp.zeros((GROUPS, SLOTS), F32)
    low_part = jnp.zeros((GROUPS, SLOTS), F32)
    for j in range(2):
        slot = onehot(s_iota == ranks[j].astype(I32))
        v1 = (tok // 8).astype(F32)
        v2 = ((tok % 8) * 32 + kind_ref[...]).astype(F32)
        high = high + mm(owners[j], (slot.astype(F32) * v1).astype(BF16), NT)
        low_part = low_part + mm(owners[j], (slot.astype(F32) * v2).astype(BF16), NT)
        at = jnp.sum(owners[j].astype(F32) * offset, axis=0, keepdims=True) + ranks[j]
        rho_ref[j : j + 1, :] = at.astype(I32)
    low_int = low_part.astype(I32)
    kinds = low_int % 32
    token = high.astype(I32) * 8 + low_int // 32
    s_lane = iota((GROUPS, SLOTS), 1)
    live = s_lane < count.astype(I32)
    tab_ref[:, 0:SLOTS] = token + 1024 * kinds
    extra = jnp.where(s_lane == 0, offset * 0.125, count)
    tab_ref[:, SLOTS : 2 * SLOTS] = extra.astype(I32)
    kinds_ref[:, 0:SLOTS] = jnp.where(live, kinds, -1)
    kinds_ref[:, SLOTS : 2 * SLOTS] = jnp.full((GROUPS, SLOTS), -1, I32)


def turn_pixels(part_ref, xs_ref, perm, begin, end):
    def make_perm(i, _):
        r = iota((64, PIX), 0)
        c = iota((64, PIX), 1)
        hit = c == (r * CYC + i)
        perm[pl.ds(pl.multiple_of(i * 64, 64), 64), :] = onehot(hit)
        return 0

    if begin == 0:
        lax.fori_loop(0, CYC, make_perm, 0)

    def turn_rows(i, _):
        y = mm(part_ref[pl.ds(pl.multiple_of(i * 128, 128), 128), :], perm[...])
        for j in range(8):
            xs_ref[pl.ds(i * 1024 + j, 128, stride=8), :] = y[:, j * 128 : (j + 1) * 128]
        return 0

    lax.fori_loop(begin, end, turn_rows, 0)


def start_kernel(cand_ref, kind_ref, mine_ref, part_ref, tab_ref, kinds_ref, rho_ref, pack_ref, all_ref, xs_ref, perm, send_sem, recv_sem, own_sem):
    me = lax.axis_index("dom")
    row = lax.axis_index("cls")
    z, x, core = me // 8, (me // 2) % X, me % 2

    def peer(n):
        if n < 7:
            return lax.rem(z + n + 1, Z) * 8 + x * 2 + core
        if n < 10:
            return z * 8 + lax.rem(x + n - 6, X) * 2 + core
        return z * 8 + x * 2 + (1 - core)

    barrier = pltpu.get_barrier_semaphore()
    for n in range(11):
        pl.semaphore_signal(barrier, inc=1, device_id=(row, peer(n)), device_id_type=MESH)
    pl.semaphore_wait(barrier, 11)

    def copy(n):
        if n < 7:
            src, dst = mine_ref, all_ref.at[z, x, core]
        elif n < 10:
            src = dst = all_ref.at[:, x, core]
        else:
            src = dst = all_ref.at[:, :, core]
        return pltpu.make_async_remote_copy(
            src_ref=src,
            dst_ref=dst,
            send_sem=send_sem.at[n],
            recv_sem=recv_sem.at[n],
            device_id=(row, peer(n)),
            device_id_type=MESH,
        )

    first = [copy(n) for n in range(7)]
    second = [copy(n) for n in range(7, 10)]
    third = copy(10)
    for c in first:
        c.start()
    own = pltpu.make_async_copy(mine_ref, all_ref.at[z, x, core], own_sem)
    own.start()
    route(me, cand_ref, kind_ref, tab_ref, kinds_ref, rho_ref, pack_ref)
    own.wait()
    for c in first:
        c.wait()
    for c in second:
        c.start()
    turn_pixels(part_ref, xs_ref, perm, 0, 4)
    for c in second:
        c.wait()
    third.start()
    turn_pixels(part_ref, xs_ref, perm, 4, 8)
    third.wait()


def start_stage(cand_t, kinds_row, mine, particles):
    return pl.pallas_call(
        start_kernel,
        out_shape=(
            jax.ShapeDtypeStruct((GROUPS, 2 * SLOTS), I32),
            jax.ShapeDtypeStruct((GROUPS, 2 * SLOTS), I32),
            jax.ShapeDtypeStruct((2, TOK), I32),
            jax.ShapeDtypeStruct((1, 384), I32),
            jax.ShapeDtypeStruct((Z, X, 2, 32, 128), BF16),
            jax.ShapeDtypeStruct((TOK * 8, 128), F32),
        ),
        in_specs=vm(4),
        out_specs=tuple(vm(6)),
        scratch_shapes=[
            pltpu.VMEM((PIX, PIX), BF16),
            pltpu.SemaphoreType.DMA((11,)),
            pltpu.SemaphoreType.DMA((11,)),
            pltpu.SemaphoreType.DMA,
        ],
        compiler_params=pltpu.CompilerParams(collective_id=0, has_side_effects=True, vmem_limit_bytes=VMEM_LIMIT),
        name="start_stage",
    )(cand_t, kinds_row, mine, particles)


def ring_hop(ring, n, k, to, dom, src, dst):
    return pltpu.make_async_remote_copy(
        src_ref=src,
        dst_ref=dst,
        send_sem=ring.at[0, n, k],
        recv_sem=ring.at[1, n, k],
        device_id=(to, dom),
        device_id_type=MESH,
    )


def score_kernel(tab_ref, pack_ref, xs, refs_ref, rott_ref, ctf_ref, kinds_ref, total_ref, wout_ref, cs, power, bd, raw, rot_a, rot_b, stage_a, stage_b, hits_a, hits_b, wall, table, packed, far, held, near, ring, out_sem):
    rots, stages, hits = (rot_a, rot_b), (stage_a, stage_b), (hits_a, hits_b)
    me = lax.axis_index("cls")
    dom = lax.axis_index("dom")
    right, left, across = lax.rem(me + 1, SHARES), lax.rem(me + 3, SHARES), lax.rem(me + 2, SHARES)
    low, high = pl.ds(0, 32), pl.ds(32, 32)
    barrier = pltpu.get_barrier_semaphore()
    for to in (right, left):
        pl.semaphore_signal(barrier, inc=1, device_id=(to, dom), device_id_type=MESH)
    pl.semaphore_wait(barrier, 2)

    def outgoing(k):
        return (
            ring_hop(ring, 0, k, right, dom, packed.at[k, across, low], far.at[k, 0]),
            ring_hop(ring, 1, k, left, dom, packed.at[k, across, high], far.at[k, 1]),
            ring_hop(ring, 2, k, right, dom, packed.at[k, right, high], near.at[k, 0, high]),
            ring_hop(ring, 3, k, left, dom, packed.at[k, left, low], near.at[k, 1, low]),
        )

    def relayed(k):
        return (
            ring_hop(ring, 4, k, right, dom, held.at[k, 0], near.at[k, 0, low]),
            ring_hop(ring, 5, k, left, dom, held.at[k, 1], near.at[k, 1, high]),
        )

    def pack(k):
        for q in range(SHARES):
            for j in range(8):
                src = pack_ref[0, k * 32 + q * 8 + j]
                packed[k, q, j * 8 : (j + 1) * 8, :] = table[src]
        for c in outgoing(k):
            c.start()

    def relay(k):
        c0, c1, _, _ = outgoing(k)
        c0.wait()
        c1.wait()
        held[k, 0] = packed[k, right, low, :] + far[k, 0]
        held[k, 1] = packed[k, left, high, :] + far[k, 1]
        for c in relayed(k):
            c.start()

    for j in range(8):
        cs[:, j, :] = ctf_ref[:, j * 128 : (j + 1) * 128]
    square = -0.5 * (ctf_ref[...] * ctf_ref[...])
    s1 = square.astype(BF16)
    power[0:32, :] = s1
    power[32:64, :] = (square - s1.astype(F32)).astype(BF16)
    bd[...] = jnp.zeros_like(bd)
    half = iota((1, 128), 1) < 64
    keep = jnp.broadcast_to(half, (64, 128))
    keep_16 = jnp.broadcast_to(half, (16, 128))
    blank = jnp.zeros((16, 128), BF16)
    k_row = iota((128, 128), 0)

    def rotate(pair):
        for u in range(2):
            for cl in range(2):
                x = refs_ref[lax.rem(dom + pair * 2 + u, GROUPS), cl * 16 : (cl + 1) * 16, :]
                y = pltpu.roll(x, 64, 1)
                for ch, (low, high) in enumerate(((x, y), (y, x))):
                    at = u * 256 + (ch * 2 + cl) * 64
                    low = jnp.where(keep_16, low, blank)
                    high = jnp.where(keep_16, blank, high)
                    bd[at : at + 16, 0:128] = low
                    bd[at + 16 : at + 32, 0:128] = high
                    bd[at + 32 : at + 48, 128:256] = low
                    bd[at + 48 : at + 64, 128:256] = high
        for n in range(4):
            at = slice(n * 256, (n + 1) * 256)
            raw[:, at] = mm(bd[...], rott_ref[:, at]).astype(BF16)

    def arrange(pair, u):
        g = pair * 2 + u
        rot, stage = rots[u], stages[u]
        for s in range(SLOTS):
            entry = tab_ref[g, s]
            stage[s * 8 : (s + 1) * 8, :] = xs[entry & 1023] * cs[lax.shift_right_logical(entry, 10)]
        for qp in range(8):
            for k in range(2):
                r0 = u * 256 + k * 128
                a = raw[r0 : r0 + 64, qp * 128 : (qp + 1) * 128]
                b = raw[r0 + 64 : r0 + 128, qp * 128 : (qp + 1) * 128]
                rot[qp * 128 : qp * 128 + 64, k * 128 : (k + 1) * 128] = jnp.where(keep, a, pltpu.roll(b, 64, 1))
                rot[qp * 128 + 64 : qp * 128 + 128, k * 128 : (k + 1) * 128] = jnp.where(keep, pltpu.roll(a, 64, 1), b)
        for j in range(8):
            col = stage[pl.ds(j, SLOTS, stride=8), :].astype(BF16)
            wall[g, :, j * 128 : (j + 1) * 128] = col
        kinds = kinds_ref[pl.ds(g, 1), :]
        hit = jnp.where(((k_row & 31) == kinds) & (k_row < 64), 1.0, 0.0)
        hits[u][...] = jnp.transpose(hit)[0:SLOTS, :].astype(BF16)

    def score(pair, u):
        g = pair * 2 + u
        rot = rots[u]
        en, total = None, None
        for part in range(2):
            at = slice(part * 512, (part + 1) * 512)
            r = rot[at, :]
            z = mm(wall[g, :, at], r)
            y = mm(power[:, at], r * r)
            total = z if total is None else total + z
            en = y if en is None else en + y
        en = en[0:32, :] + en[32:64, :]
        p1 = en.astype(BF16)
        p2 = (en - p1.astype(F32)).astype(BF16)
        total = total + mm(hits[u][:, 0:64], jnp.concatenate([p1, p2], axis=0))
        table[pl.ds(g * 8, 8)] = (total * (4.0 / 64.0)).reshape(8, 8, PAIRS)

    def saved(g):
        return pltpu.make_async_copy(wall.at[g], wout_ref.at[g], out_sem.at[g])

    def step(t, _):
        for u in range(2):
            score(jnp.clip(t - 2, 0, PAIRS_OF - 1), u)
        for u in range(2):
            arrange(jnp.clip(t - 1, 0, PAIRS_OF - 1), u)
        rotate(jnp.minimum(t, PAIRS_OF - 1))
        return 0

    lax.fori_loop(0, 18, step, 0)

    def chunk(k, _):
        lax.fori_loop(18 + 2 * k, 20 + 2 * k, step, 0)
        pack(k)

        @pl.when(k > 0)
        def _():
            relay(k - 1)

        return 0

    lax.fori_loop(0, 8, chunk, 0)

    def save(g, _):
        saved(g).start()
        return 0

    pack(8)
    relay(7)
    pack(9)
    relay(8)
    lax.fori_loop(0, GROUPS, save, 0)
    relay(9)

    def finish(k, _):
        _, _, c2, c3 = outgoing(k)
        c4, c5 = relayed(k)
        for c in (c2, c3, c4, c5):
            c.wait()
        total_ref[k] = packed[k, me] + near[k, 0] + near[k, 1]
        return 0

    lax.fori_loop(0, CHUNKS, finish, 0)

    def save_end(g, _):
        saved(g).wait()
        return 0

    lax.fori_loop(0, GROUPS, save_end, 0)


def score_stage(tab, packing, xs, refs, rott, ctf, kinds):
    return pl.pallas_call(
        score_kernel,
        out_shape=(
            jax.ShapeDtypeStruct((CHUNKS, 64, PAIRS), F32),
            jax.ShapeDtypeStruct((GROUPS, SLOTS, PIX), BF16),
        ),
        in_specs=[pl.BlockSpec(memory_space=pltpu.SMEM)] * 2 + vm(5),
        out_specs=(pl.BlockSpec(memory_space=pltpu.VMEM), pl.BlockSpec(memory_space=pl.ANY)),
        scratch_shapes=[
            pltpu.VMEM((KINDS, 8, 128), F32),
            pltpu.VMEM((64, PIX), BF16),
            pltpu.VMEM((512, 256), BF16),
            pltpu.VMEM((512, PIX), BF16),
            pltpu.VMEM((PIX, PAIRS), BF16),
            pltpu.VMEM((PIX, PAIRS), BF16),
            pltpu.VMEM((SLOTS * 8, 128), F32),
            pltpu.VMEM((SLOTS * 8, 128), F32),
            pltpu.VMEM((SLOTS, 128), BF16),
            pltpu.VMEM((SLOTS, 128), BF16),
            pltpu.VMEM((GROUPS, SLOTS, PIX), BF16),
            pltpu.VMEM((GROUPS * 8, 8, PAIRS), F32),
            pltpu.VMEM((CHUNKS, SHARES, 64, PAIRS), F32),
            pltpu.VMEM((CHUNKS, 2, 32, PAIRS), F32),
            pltpu.VMEM((CHUNKS, 2, 32, PAIRS), F32),
            pltpu.VMEM((CHUNKS, 2, 64, PAIRS), F32),
            pltpu.SemaphoreType.DMA((2, 6, CHUNKS)),
            pltpu.SemaphoreType.DMA((GROUPS,)),
        ],
        compiler_params=pltpu.CompilerParams(collective_id=1, has_side_effects=True, vmem_limit_bytes=VMEM_LIMIT),
        name="score_stage",
    )(tab, packing, xs.reshape(TOK, 8, 128), refs.reshape(GROUPS, 32, 128), rott, ctf, kinds)


def turned(raw, rsq):
    keep = jnp.broadcast_to(iota((1, 128), 1) < 64, (64, 128))
    for qp in range(8):
        for c in range(2):
            a = raw[c * 128 : c * 128 + 64, qp * 128 : (qp + 1) * 128]
            b = raw[c * 128 + 64 : c * 128 + 128, qp * 128 : (qp + 1) * 128]
            e = jnp.where(keep, a, pltpu.roll(b, 64, 1))
            o = jnp.where(keep, pltpu.roll(a, 64, 1), b)
            rsq[qp * 128 : qp * 128 + 64, c * 128 : (c + 1) * 128] = e
            rsq[qp * 128 + 64 : qp * 128 + 128, c * 128 : (c + 1) * 128] = o


def diagonal(rott_ref, rsq):
    lane = iota((1, 256), 1)
    total = None
    for part in range(2):
        at = slice(part * 512, (part + 1) * 512)
        full = mm(rott_ref[:, at], rsq[at, :])
        diag = full[0:64, :]
        for b in range(1, 4):
            diag = jnp.where((lane // CYC) % 4 == b, full[b * 64 : (b + 1) * 64, :], diag)
        total = diag if total is None else total + diag
    return total


def folds():
    ri = iota((256, 128), 0)
    ci = iota((256, 128), 1)
    want = (ri // 64) * CYC + ri % CYC
    return [onehot(ci == want + 64 * h) for h in range(2)]


def folded(parts, fold):
    out = None
    for x, f in zip(parts, fold):
        p1 = x.astype(BF16)
        p2 = (x - p1.astype(F32)).astype(BF16)
        y = mm(p1, f) + mm(p2, f)
        out = y if out is None else out + y
    return out


def tail_kernel(tab_ref, kinds_ref, rho_ref, total_ref, rott_ref, ctf_ref, wout_ref, cs_ref, cw_ref, log_ref, weighted, w_ref, wide, stat, stat_recv, rsq_a, rsq_b, raw_a, raw_b, parts, msg, got, mine, others, ring, stat_sem, ssem, rsem, share_sem, load_sem):
    rsqs, raws = (rsq_a, rsq_b), (raw_a, raw_b)
    me = lax.axis_index("cls")
    dom = lax.axis_index("dom")
    right, left = lax.rem(me + 1, SHARES), lax.rem(me + 3, SHARES)
    low, high = pl.ds(0, 32), pl.ds(32, 32)
    load = pltpu.make_async_copy(wout_ref, weighted, load_sem)
    load.start()
    barrier = pltpu.get_barrier_semaphore()
    for d in range(1, SHARES):
        pl.semaphore_signal(barrier, inc=1, device_id=(lax.rem(me + d, SHARES), dom), device_id_type=MESH)

    def greet(i, _):
        pl.semaphore_signal(barrier, inc=1, device_id=(me, lax.rem(dom + i, GROUPS)), device_id_type=MESH)
        return 0

    lax.fori_loop(1, GROUPS, greet, 0)
    lanes = iota((64, 128), 1)
    top = jnp.zeros((64, 128), F32)
    tot = jnp.zeros((64, 128), F32)
    for k in range(CHUNKS):
        x = total_ref[k]
        m = jnp.max(x, axis=1, keepdims=True)
        s = jnp.sum(jnp.exp(x - m), axis=1, keepdims=True)
        here = lanes == 4 * k + me
        top = jnp.where(here, m, top)
        tot = jnp.where(here, s, tot)
    stat[0] = top
    stat[1] = tot
    pl.semaphore_wait(barrier, GROUPS - 1 + SHARES - 1)

    def to_peer(sem, d, src, dst):
        return pltpu.make_async_remote_copy(
            src_ref=src,
            dst_ref=dst,
            send_sem=sem.at[0, d],
            recv_sem=sem.at[1, d],
            device_id=(lax.rem(me + d, SHARES), dom),
            device_id_type=MESH,
        )

    swaps = [to_peer(stat_sem, d, stat, stat_recv.at[d - 1]) for d in (2, 1, 3)]
    for c in swaps:
        c.start()
    his, los = [], []
    for j in range(2):
        rho = rho_ref[j : j + 1, :]
        his.append(onehot(iota((128, TOK), 0) == lax.shift_right_logical(rho, 6)))
        los.append(jnp.where(iota((64, TOK), 0) == (rho & 63), 1.0, 0.0))
    for c in swaps:
        c.wait()
    top = stat[0] + stat_recv[0, 0] + stat_recv[1, 0] + stat_recv[2, 0]
    tot = stat[1] + stat_recv[0, 1] + stat_recv[1, 1] + stat_recv[2, 1]
    three = jnp.concatenate(list(pieces(top)) + list(pieces(tot)), axis=0)
    maxima, sums = [], []
    for j in range(2):
        t = mm(three, his[j])
        maxima.append(jnp.sum((t[0:64] + t[64:128] + t[128:192]) * los[j], axis=0, keepdims=True))
        sums.append(jnp.sum((t[192:256] + t[256:320] + t[320:384]) * los[j], axis=0, keepdims=True))
    best = jnp.maximum(maxima[0], maxima[1])
    log = best + jnp.log(sums[0] * jnp.exp(maxima[0] - best) + sums[1] * jnp.exp(maxima[1] - best))
    log_ref[...] = log
    back = jnp.zeros((64, 128), F32)
    for j in range(2):
        for p in pieces(log):
            back = back + mm((los[j] * p.astype(F32)).astype(BF16), his[j], NT)
    for k in range(CHUNKS):
        col = jnp.sum(jnp.where(lanes == 4 * k + me, back, 0.0), axis=1, keepdims=True)
        w_ref[k, me] = jnp.exp(total_ref[k] - col).astype(BF16)

    def own(k):
        return (
            ring_hop(ring, 0, k, right, dom, w_ref.at[k, me], w_ref.at[k, me]),
            ring_hop(ring, 1, k, left, dom, w_ref.at[k, me], w_ref.at[k, me]),
        )

    def forward(k):
        return (
            ring_hop(ring, 2, k, right, dom, w_ref.at[k, left, low], w_ref.at[k, left, low]),
            ring_hop(ring, 3, k, left, dom, w_ref.at[k, right, high], w_ref.at[k, right, high]),
        )

    def begin(copies):
        for c in copies:
            c.start()

    def end(copies):
        for c in copies:
            c.wait()

    for k in range(3):
        begin(own(k))
    end(own(0))
    begin(forward(0))
    load.wait()
    s_col = iota((SLOTS, PAIRS), 0)
    k_col = iota((8, 128), 0) + me * 8
    fold = folds()

    def spread_out(pair, u, raw):
        g = pair * 2 + u
        at = tab_ref[g, SLOTS]
        w = jnp.concatenate([wide[at + j] for j in range(8)], axis=0)
        w = jnp.where(s_col < tab_ref[g, SLOTS + 1], w, 0.0)
        wt = jnp.transpose(w).astype(BF16)
        for n in range(4):
            at = slice(n * 256, (n + 1) * 256)
            raw[:, at] = mm(wt, weighted[g, :, at]).astype(BF16)
        kinds = kinds_ref[pl.ds(g, 1), :]
        hit = onehot(k_col == kinds)[:, 0:SLOTS]
        pk = mm(hit, w.astype(BF16))
        msg[g, 32:48, :] = jnp.concatenate([pk[:, 0:128], pk[:, 128:256]], axis=0).astype(BF16)

    def fold_pair(pair):
        out = folded([parts[h] for h in range(2)], fold).astype(BF16)
        for u in range(2):
            msg[pair * 2 + u, 0:32, :] = out[u * 32 : (u + 1) * 32, :]

    def to_owner(i):
        return pltpu.make_async_remote_copy(
            src_ref=msg.at[i],
            dst_ref=got.at[i],
            send_sem=ssem.at[i],
            recv_sem=rsem.at[i],
            device_id=(me, lax.rem(dom + i, GROUPS)),
            device_id_type=MESH,
        )

    def step(t, _):
        @pl.when(t > 4)
        def _():
            to_owner(2 * (t - 4)).start()

        @pl.when(t > 3)
        def _():
            to_owner(2 * (t - 4) + 1).start()

        fold_pair(jnp.clip(t - 3, 0, PAIRS_OF - 1))
        for u in range(2):
            diag = diagonal(rott_ref, rsqs[u])
            for h in range(2):
                parts[h, u * 32 : (u + 1) * 32, :] = diag[h * 32 : (h + 1) * 32, :]
        for u in range(2):
            turned(raws[u], rsqs[u])
        for u in range(2):
            spread_out(jnp.minimum(t, PAIRS_OF - 1), u, raws[u])
        return 0

    def chunk(k, _):
        @pl.when(k + 3 < CHUNKS)
        def _():
            begin(own(k + 3))

        @pl.when(k + 1 < CHUNKS)
        def _():
            end(own(k + 1))
            begin(forward(k + 1))

        end(forward(k))
        for q in range(SHARES):
            wide[pl.ds(k * 32 + q * 8, 8)] = w_ref[k, q].astype(F32).reshape(8, 8, PAIRS)
        lax.fori_loop(2 * k, 2 * k + 2, step, 0)
        return 0

    lax.fori_loop(0, CHUNKS, chunk, 0)
    lax.fori_loop(2 * CHUNKS, PAIRS_OF + 3, step, 0)
    for u in range(2):
        to_owner(GROUPS - 2 + u).start()

    def arrive(i, acc):
        to_owner(i).wait()
        return acc + got[i].astype(F32)

    acc = lax.fori_loop(1, GROUPS, arrive, msg[0].astype(F32))
    mine[...] = acc[32:48, :]
    shares = [to_peer(share_sem, d, mine, others.at[d - 1]) for d in range(1, SHARES)]
    for c in shares:
        c.start()

    def placed(x, ref):
        t = jnp.transpose(x)
        ref[:, 0:32] = t[0:64, :].astype(ref.dtype)
        ref[:, 32:64] = t[64:128, :].astype(ref.dtype)

    placed(acc[0:32, :], cs_ref)
    for c in shares:
        c.wait()
    rows = []
    for k in range(SHARES):
        x = mine[...]
        for d in range(1, SHARES):
            x = jnp.where(lax.rem(k + d, SHARES) == me, others[d - 1], x)
        rows.append(jnp.concatenate([x[0:8, :], x[8:16, :]], axis=1))
    pkt = jnp.transpose(jnp.concatenate(rows, axis=0))
    power = ctf_ref[...] * ctf_ref[...]
    for n in range(4):
        at = slice(n * 256, (n + 1) * 256)
        raw_a[:, at] = lax.dot_general(
            pkt, power[:, at], NN, precision=lax.Precision.HIGHEST, preferred_element_type=F32
        ).astype(BF16)
    turned(raw_a, rsq_a)
    diag = diagonal(rott_ref, rsq_a)
    placed(folded([diag[0:32], diag[32:64]], folds()), cw_ref)


def tail_stage(tab, kinds, rho, total, rott, ctf, weighted):
    return pl.pallas_call(
        tail_kernel,
        out_shape=(
            jax.ShapeDtypeStruct((64, 64), BF16),
            jax.ShapeDtypeStruct((64, 64), F32),
            jax.ShapeDtypeStruct((1, TOK), F32),
        ),
        in_specs=[pl.BlockSpec(memory_space=pltpu.SMEM)] + vm(5) + [pl.BlockSpec(memory_space=pl.ANY)],
        out_specs=tuple(vm(3)),
        scratch_shapes=[
            pltpu.VMEM((GROUPS, SLOTS, PIX), BF16),
            pltpu.VMEM((CHUNKS, SHARES, 64, PAIRS), BF16),
            pltpu.VMEM((PACKED // 8, 8, PAIRS), F32),
            pltpu.VMEM((2, 64, 128), F32),
            pltpu.VMEM((SHARES - 1, 2, 64, 128), F32),
            pltpu.VMEM((1024, 256), BF16),
            pltpu.VMEM((1024, 256), BF16),
            pltpu.VMEM((PAIRS, PIX), BF16),
            pltpu.VMEM((PAIRS, PIX), BF16),
            pltpu.VMEM((2, 64, 256), F32),
            pltpu.VMEM((GROUPS, 48, 128), BF16),
            pltpu.VMEM((GROUPS, 48, 128), BF16),
            pltpu.VMEM((16, 128), F32),
            pltpu.VMEM((SHARES - 1, 16, 128), F32),
            pltpu.SemaphoreType.DMA((2, 4, CHUNKS)),
            pltpu.SemaphoreType.DMA((2, SHARES)),
            pltpu.SemaphoreType.DMA((GROUPS,)),
            pltpu.SemaphoreType.DMA((GROUPS,)),
            pltpu.SemaphoreType.DMA((2, SHARES)),
            pltpu.SemaphoreType.DMA,
        ],
        compiler_params=pltpu.CompilerParams(collective_id=2, has_side_effects=True, vmem_limit_bytes=VMEM_LIMIT),
        name="tail_stage",
    )(tab, kinds, rho, total, rott, ctf, weighted)


def prepared(candidates, defocus, ctf_table, references, rotations):
    mine = references.reshape(2, 2, CYC, ANG).transpose(1, 2, 0, 3).reshape(32, 128)
    rott = rotations.reshape(ROT, CYC, 4 * ANG).transpose(2, 1, 0).reshape(256, 1024)
    ctf = ctf_table.reshape(KINDS, CYC, ANG).transpose(0, 2, 1).reshape(KINDS, PIX)
    return mine, rott, ctf, candidates.T, defocus.reshape(1, TOK)


def local(particles, candidates, defocus, ctf_table, references, rotations):
    mine, rott, ctf, cand_t, kinds_row = prepared(candidates, defocus, ctf_table, references, rotations)
    tab, kinds, rho, packing, refs, xs = start_stage(cand_t, kinds_row, mine, particles)
    total, weighted = score_stage(tab, packing, xs, refs, rott, ctf, kinds)
    cs, cw, log = tail_stage(tab, kinds, rho, total, rott, ctf, weighted)
    return cs.reshape(CPG, PIX), cw.reshape(CPG, PIX), log.reshape(TOK)


def solution(mesh):
    in_specs = (P("dom", "cls"), P("dom", None), P("dom"), P(None, "cls"), P("dom", "cls"), P())
    out_specs = (P("dom", "cls"), P("dom", "cls"), P("dom"))
    return jax.shard_map(local, mesh=mesh, in_specs=in_specs, out_specs=out_specs, check_vma=False)
```

```python
import functools

import jax
import jax.numpy as jnp
from jax import lax
from jax.experimental import pallas as pl
from jax.experimental.pallas import tpu as pltpu
from jax.sharding import PartitionSpec as P

F32 = jnp.float32
BF16 = jnp.bfloat16
I32 = jnp.int32
MESH = pl.DeviceIdType.MESH
NT = (((1,), (1,)), ((), ()))
NN = (((1,), (0,)), ((), ()))

GROUPS = 64
SLOTS = 64
ANG = 64
CYC = 16
CPG = 4
ROT = 64
PAIRS = CPG * ROT
PIX = CYC * ANG
KINDS = 32
TOK = 1024
SHARES = 4
ROWS = 640
PACKED = SHARES * ROWS
CHUNKS = ROWS // 64
PAIRS_OF = GROUPS // 2
Z, X = 8, 4
VMEM_LIMIT = 60 * 1024 * 1024


def mm(a, b, dims=NN):
    return lax.dot_general(a, b, dims, preferred_element_type=F32)


def iota(shape, dim):
    return lax.broadcasted_iota(I32, shape, dim)


def pieces(x):
    p1 = x.astype(BF16)
    r1 = x - p1.astype(F32)
    p2 = r1.astype(BF16)
    p3 = (r1 - p2.astype(F32)).astype(BF16)
    return p1, p2, p3


def onehot(mask):
    return jnp.where(mask, 1.0, 0.0).astype(BF16)


def owner_of(dom, i):
    return lax.rem(dom + (i % 8) * 8 + i // 8, GROUPS)


def vm(n):
    return [pl.BlockSpec(memory_space=pltpu.VMEM)] * n


def route(me, cand_ref, kind_ref, tab_ref, kinds_ref, rho_ref, pack_ref):
    g_iota = iota((GROUPS, TOK), 0)
    tri = onehot(iota((256, 256), 0) < iota((256, 256), 1))
    count = jnp.zeros((GROUPS, 1), F32)
    owners, ranks = [], []
    for j in range(2):
        shift = (cand_ref[j : j + 1, :] - me) & (GROUPS - 1)
        owner = onehot(g_iota == ((shift & 7) * 8 + lax.shift_right_logical(shift, 3)))
        owners.append(owner)
        row = []
        for blk in range(TOK // 256):
            part = owner[:, blk * 256 : (blk + 1) * 256]
            before = mm(part, tri) + count
            row.append(jnp.sum(before * part.astype(F32), axis=0, keepdims=True))
            count = count + jnp.sum(part.astype(F32), axis=1, keepdims=True)
        ranks.append(jnp.concatenate(row, axis=1))
    padded = jnp.floor((count + 7.0) * 0.125) * 8.0
    low = onehot(iota((GROUPS, GROUPS), 1) < iota((GROUPS, GROUPS), 0))
    offset = mm(low, jnp.broadcast_to(padded, (GROUPS, 128)).astype(BF16))[:, 0:1]
    at = iota((GROUPS, 384), 1) * 8
    ended = jnp.where(at >= (offset + padded).astype(I32), 1, 0)
    where_in = jnp.sum(ended, axis=0, keepdims=True)
    first = jnp.sum(jnp.where(iota((GROUPS, 384), 0) == where_in, offset.astype(I32), 0), axis=0, keepdims=True)
    source = where_in * 8 + (iota((1, 384), 1) - lax.shift_right_logical(first, 3))
    pack_ref[...] = jnp.where(where_in < GROUPS, source, 0)
    tok = iota((1, TOK), 1)
    s_iota = iota((SLOTS, TOK), 0)
    high = jnp.zeros((GROUPS, SLOTS), F32)
    low_part = jnp.zeros((GROUPS, SLOTS), F32)
    for j in range(2):
        slot = onehot(s_iota == ranks[j].astype(I32))
        v1 = (tok // 8).astype(F32)
        v2 = ((tok % 8) * 32 + kind_ref[...]).astype(F32)
        high = high + mm(owners[j], (slot.astype(F32) * v1).astype(BF16), NT)
        low_part = low_part + mm(owners[j], (slot.astype(F32) * v2).astype(BF16), NT)
        at = jnp.sum(owners[j].astype(F32) * offset, axis=0, keepdims=True) + ranks[j]
        rho_ref[j : j + 1, :] = at.astype(I32)
    low_int = low_part.astype(I32)
    kinds = low_int % 32
    token = high.astype(I32) * 8 + low_int // 32
    s_lane = iota((GROUPS, SLOTS), 1)
    live = s_lane < count.astype(I32)
    tab_ref[:, 0:SLOTS] = token + 1024 * kinds
    extra = jnp.where(s_lane == 0, offset * 0.125, count)
    tab_ref[:, SLOTS : 2 * SLOTS] = extra.astype(I32)
    kinds_ref[:, 0:SLOTS] = jnp.where(live, kinds, -1)
    kinds_ref[:, SLOTS : 2 * SLOTS] = jnp.full((GROUPS, SLOTS), -1, I32)


def turn_pixels(part_ref, xs_ref, perm, begin, end):
    def make_perm(i, _):
        r = iota((64, PIX), 0)
        c = iota((64, PIX), 1)
        hit = c == (r * CYC + i)
        perm[pl.ds(pl.multiple_of(i * 64, 64), 64), :] = onehot(hit)
        return 0

    if begin == 0:
        lax.fori_loop(0, CYC, make_perm, 0)

    def turn_rows(i, _):
        y = mm(part_ref[pl.ds(pl.multiple_of(i * 128, 128), 128), :], perm[...])
        for j in range(8):
            xs_ref[pl.ds(i * 1024 + j, 128, stride=8), :] = y[:, j * 128 : (j + 1) * 128]
        return 0

    lax.fori_loop(begin, end, turn_rows, 0)


def start_kernel(cand_ref, kind_ref, mine_ref, part_ref, tab_ref, kinds_ref, rho_ref, pack_ref, all_ref, xs_ref, perm, send_sem, recv_sem, own_sem):
    me = lax.axis_index("dom")
    row = lax.axis_index("cls")
    z, x, core = me // 8, (me // 2) % X, me % 2

    def peer(n):
        if n < 7:
            return lax.rem(z + n + 1, Z) * 8 + x * 2 + core
        if n < 10:
            return z * 8 + lax.rem(x + n - 6, X) * 2 + core
        return z * 8 + x * 2 + (1 - core)

    barrier = pltpu.get_barrier_semaphore()
    for n in range(11):
        pl.semaphore_signal(barrier, inc=1, device_id=(row, peer(n)), device_id_type=MESH)
    pl.semaphore_wait(barrier, 11)

    def copy(n):
        if n < 7:
            src, dst = mine_ref, all_ref.at[z, x, core]
        elif n < 10:
            src = dst = all_ref.at[:, x, core]
        else:
            src = dst = all_ref.at[:, :, core]
        return pltpu.make_async_remote_copy(
            src_ref=src,
            dst_ref=dst,
            send_sem=send_sem.at[n],
            recv_sem=recv_sem.at[n],
            device_id=(row, peer(n)),
            device_id_type=MESH,
        )

    first = [copy(n) for n in range(7)]
    second = [copy(n) for n in range(7, 10)]
    third = copy(10)
    for c in first:
        c.start()
    own = pltpu.make_async_copy(mine_ref, all_ref.at[z, x, core], own_sem)
    own.start()
    route(me, cand_ref, kind_ref, tab_ref, kinds_ref, rho_ref, pack_ref)
    own.wait()
    for c in first:
        c.wait()
    for c in second:
        c.start()
    turn_pixels(part_ref, xs_ref, perm, 0, 4)
    for c in second:
        c.wait()
    third.start()
    turn_pixels(part_ref, xs_ref, perm, 4, 8)
    third.wait()


def start_stage(cand_t, kinds_row, mine, particles):
    return pl.pallas_call(
        start_kernel,
        out_shape=(
            jax.ShapeDtypeStruct((GROUPS, 2 * SLOTS), I32),
            jax.ShapeDtypeStruct((GROUPS, 2 * SLOTS), I32),
            jax.ShapeDtypeStruct((2, TOK), I32),
            jax.ShapeDtypeStruct((1, 384), I32),
            jax.ShapeDtypeStruct((Z, X, 2, 32, 128), BF16),
            jax.ShapeDtypeStruct((TOK * 8, 128), F32),
        ),
        in_specs=vm(4),
        out_specs=tuple(vm(6)),
        scratch_shapes=[
            pltpu.VMEM((PIX, PIX), BF16),
            pltpu.SemaphoreType.DMA((11,)),
            pltpu.SemaphoreType.DMA((11,)),
            pltpu.SemaphoreType.DMA,
        ],
        compiler_params=pltpu.CompilerParams(collective_id=0, has_side_effects=True, vmem_limit_bytes=VMEM_LIMIT),
        name="start_stage",
    )(cand_t, kinds_row, mine, particles)


def turned(raw, rsq):
    keep = jnp.broadcast_to(iota((1, 128), 1) < 64, (64, 128))
    for qp in range(8):
        for c in range(2):
            a = raw[c * 128 : c * 128 + 64, qp * 128 : (qp + 1) * 128]
            b = raw[c * 128 + 64 : c * 128 + 128, qp * 128 : (qp + 1) * 128]
            e = jnp.where(keep, a, pltpu.roll(b, 64, 1))
            o = jnp.where(keep, pltpu.roll(a, 64, 1), b)
            rsq[qp * 128 : qp * 128 + 64, c * 128 : (c + 1) * 128] = e
            rsq[qp * 128 + 64 : qp * 128 + 128, c * 128 : (c + 1) * 128] = o


def diagonal(rott_ref, rsq):
    lane = iota((1, 256), 1)
    total = None
    for part in range(2):
        at = slice(part * 512, (part + 1) * 512)
        full = mm(rott_ref[:, at], rsq[at, :])
        diag = full[0:64, :]
        for b in range(1, 4):
            diag = jnp.where((lane // CYC) % 4 == b, full[b * 64 : (b + 1) * 64, :], diag)
        total = diag if total is None else total + diag
    return total


def folds():
    ri = iota((256, 128), 0)
    ci = iota((256, 128), 1)
    want = (ri // 64) * CYC + ri % CYC
    return [onehot(ci == want + 64 * h) for h in range(2)]


def folded(parts, fold):
    out = None
    for x, f in zip(parts, fold):
        p1 = x.astype(BF16)
        p2 = (x - p1.astype(F32)).astype(BF16)
        y = mm(p1, f) + mm(p2, f)
        out = y if out is None else out + y
    return out


def ring_hop(ring, n, k, to, dom, src, dst):
    return pltpu.make_async_remote_copy(
        src_ref=src,
        dst_ref=dst,
        send_sem=ring.at[0, n, k],
        recv_sem=ring.at[1, n, k],
        device_id=(to, dom),
        device_id_type=MESH,
    )


def main_kernel(tab_ref, pack_ref, xs, refs_ref, rott_ref, ctf_ref, kinds_ref, rho_ref, sums_ref, pk_ref, log_ref, cs, power, bd, raw, rot_a, rot_b, stage_a, stage_b, hits_a, hits_b, wall, table, packed, far, held, near, total_ref, w_ref, wide, stat, stat_recv, rsq_a, rsq_b, raw_a, raw_b, parts, msg, got, mine, others, ring, ring2, stat_sem, ssem, rsem, share_sem):
    rots, stages, hits = (rot_a, rot_b), (stage_a, stage_b), (hits_a, hits_b)
    rsqs, raws = (rsq_a, rsq_b), (raw_a, raw_b)
    me = lax.axis_index("cls")
    dom = lax.axis_index("dom")
    right, left, across = lax.rem(me + 1, SHARES), lax.rem(me + 3, SHARES), lax.rem(me + 2, SHARES)
    low, high = pl.ds(0, 32), pl.ds(32, 32)
    barrier = pltpu.get_barrier_semaphore()
    for d in range(1, SHARES):
        pl.semaphore_signal(barrier, inc=1, device_id=(lax.rem(me + d, SHARES), dom), device_id_type=MESH)

    def greet(i, _):
        pl.semaphore_signal(barrier, inc=1, device_id=(me, lax.rem(dom + i, GROUPS)), device_id_type=MESH)
        return 0

    lax.fori_loop(1, GROUPS, greet, 0)

    def outgoing(k):
        return (
            ring_hop(ring, 0, k, right, dom, packed.at[k, across, low], far.at[k, 0]),
            ring_hop(ring, 1, k, left, dom, packed.at[k, across, high], far.at[k, 1]),
            ring_hop(ring, 2, k, right, dom, packed.at[k, right, high], near.at[k, 0, high]),
            ring_hop(ring, 3, k, left, dom, packed.at[k, left, low], near.at[k, 1, low]),
        )

    def relayed(k):
        return (
            ring_hop(ring, 4, k, right, dom, held.at[k, 0], near.at[k, 0, low]),
            ring_hop(ring, 5, k, left, dom, held.at[k, 1], near.at[k, 1, high]),
        )

    def pack(k):
        for q in range(SHARES):
            for j in range(8):
                src = pack_ref[0, k * 32 + q * 8 + j]
                packed[k, q, j * 8 : (j + 1) * 8, :] = table[src]
        for c in outgoing(k):
            c.start()

    def relay(k):
        c0, c1, _, _ = outgoing(k)
        c0.wait()
        c1.wait()
        held[k, 0] = packed[k, right, low, :] + far[k, 0]
        held[k, 1] = packed[k, left, high, :] + far[k, 1]
        for c in relayed(k):
            c.start()

    for j in range(8):
        cs[:, j, :] = ctf_ref[:, j * 128 : (j + 1) * 128]
    square = -0.5 * (ctf_ref[...] * ctf_ref[...])
    s1 = square.astype(BF16)
    power[0:32, :] = s1
    power[32:64, :] = (square - s1.astype(F32)).astype(BF16)
    bd[...] = jnp.zeros_like(bd)
    half = iota((1, 128), 1) < 64
    keep = jnp.broadcast_to(half, (64, 128))
    keep_16 = jnp.broadcast_to(half, (16, 128))
    blank = jnp.zeros((16, 128), BF16)
    k_row = iota((128, 128), 0)

    def rotate(pair):
        for u in range(2):
            for cl in range(2):
                x = refs_ref[owner_of(dom, pair * 2 + u), cl * 16 : (cl + 1) * 16, :]
                y = pltpu.roll(x, 64, 1)
                for ch, (low, high) in enumerate(((x, y), (y, x))):
                    at = u * 256 + (ch * 2 + cl) * 64
                    low = jnp.where(keep_16, low, blank)
                    high = jnp.where(keep_16, blank, high)
                    bd[at : at + 16, 0:128] = low
                    bd[at + 16 : at + 32, 0:128] = high
                    bd[at + 32 : at + 48, 128:256] = low
                    bd[at + 48 : at + 64, 128:256] = high
        for n in range(4):
            at = slice(n * 256, (n + 1) * 256)
            raw[:, at] = mm(bd[...], rott_ref[:, at]).astype(BF16)

    def arrange(pair, u):
        g = pair * 2 + u
        rot, stage = rots[u], stages[u]
        for s in range(SLOTS):
            entry = tab_ref[g, s]
            stage[s * 8 : (s + 1) * 8, :] = xs[entry & 1023] * cs[lax.shift_right_logical(entry, 10)]
        for qp in range(8):
            for k in range(2):
                r0 = u * 256 + k * 128
                a = raw[r0 : r0 + 64, qp * 128 : (qp + 1) * 128]
                b = raw[r0 + 64 : r0 + 128, qp * 128 : (qp + 1) * 128]
                rot[qp * 128 : qp * 128 + 64, k * 128 : (k + 1) * 128] = jnp.where(keep, a, pltpu.roll(b, 64, 1))
                rot[qp * 128 + 64 : qp * 128 + 128, k * 128 : (k + 1) * 128] = jnp.where(keep, pltpu.roll(a, 64, 1), b)
        for j in range(8):
            col = stage[pl.ds(j, SLOTS, stride=8), :].astype(BF16)
            wall[g, :, j * 128 : (j + 1) * 128] = col
        kinds = kinds_ref[pl.ds(g, 1), :]
        hit = jnp.where(((k_row & 31) == kinds) & (k_row < 64), 1.0, 0.0)
        hits[u][...] = jnp.transpose(hit)[0:SLOTS, :].astype(BF16)

    def score(pair, u):
        g = pair * 2 + u
        rot = rots[u]
        en, total = None, None
        for part in range(2):
            at = slice(part * 512, (part + 1) * 512)
            r = rot[at, :]
            z = mm(wall[g, :, at], r)
            y = mm(power[:, at], r * r)
            total = z if total is None else total + z
            en = y if en is None else en + y
        en = en[0:32, :] + en[32:64, :]
        p1 = en.astype(BF16)
        p2 = (en - p1.astype(F32)).astype(BF16)
        total = total + mm(hits[u][:, 0:64], jnp.concatenate([p1, p2], axis=0))
        table[pl.ds(g * 8, 8)] = (total * (4.0 / 64.0)).reshape(8, 8, PAIRS)

    def step(t, _):
        for u in range(2):
            score(jnp.clip(t - 2, 0, PAIRS_OF - 1), u)
        for u in range(2):
            arrange(jnp.clip(t - 1, 0, PAIRS_OF - 1), u)
        rotate(jnp.minimum(t, PAIRS_OF - 1))
        return 0

    lax.fori_loop(0, 18, step, 0)
    pl.semaphore_wait(barrier, GROUPS - 1 + SHARES - 1)

    def chunk(k, _):
        lax.fori_loop(18 + 2 * k, 20 + 2 * k, step, 0)
        pack(k)

        @pl.when(k > 0)
        def _():
            relay(k - 1)

        return 0

    lax.fori_loop(0, 8, chunk, 0)

    pack(8)
    relay(7)
    pack(9)
    relay(8)
    relay(9)

    def finish(k, _):
        _, _, c2, c3 = outgoing(k)
        c4, c5 = relayed(k)
        for c in (c2, c3, c4, c5):
            c.wait()
        total_ref[k] = packed[k, me] + near[k, 0] + near[k, 1]
        return 0

    lax.fori_loop(0, CHUNKS, finish, 0)

    lanes = iota((64, 128), 1)
    top = jnp.zeros((64, 128), F32)
    tot = jnp.zeros((64, 128), F32)
    for k in range(CHUNKS):
        x = total_ref[k]
        m = jnp.max(x, axis=1, keepdims=True)
        s = jnp.sum(jnp.exp(x - m), axis=1, keepdims=True)
        here = lanes == 4 * k + me
        top = jnp.where(here, m, top)
        tot = jnp.where(here, s, tot)
    stat[0] = top
    stat[1] = tot
    def to_peer(sem, d, src, dst):
        return pltpu.make_async_remote_copy(
            src_ref=src,
            dst_ref=dst,
            send_sem=sem.at[0, d],
            recv_sem=sem.at[1, d],
            device_id=(lax.rem(me + d, SHARES), dom),
            device_id_type=MESH,
        )

    swaps = [to_peer(stat_sem, d, stat, stat_recv.at[d - 1]) for d in (2, 1, 3)]
    for c in swaps:
        c.start()
    his, los = [], []
    for j in range(2):
        rho = rho_ref[j : j + 1, :]
        his.append(onehot(iota((128, TOK), 0) == lax.shift_right_logical(rho, 6)))
        los.append(jnp.where(iota((64, TOK), 0) == (rho & 63), 1.0, 0.0))
    for c in swaps:
        c.wait()
    top = stat[0] + stat_recv[0, 0] + stat_recv[1, 0] + stat_recv[2, 0]
    tot = stat[1] + stat_recv[0, 1] + stat_recv[1, 1] + stat_recv[2, 1]
    three = jnp.concatenate(list(pieces(top)) + list(pieces(tot)), axis=0)
    maxima, sums = [], []
    for j in range(2):
        t = mm(three, his[j])
        maxima.append(jnp.sum((t[0:64] + t[64:128] + t[128:192]) * los[j], axis=0, keepdims=True))
        sums.append(jnp.sum((t[192:256] + t[256:320] + t[320:384]) * los[j], axis=0, keepdims=True))
    best = jnp.maximum(maxima[0], maxima[1])
    log = best + jnp.log(sums[0] * jnp.exp(maxima[0] - best) + sums[1] * jnp.exp(maxima[1] - best))
    log_ref[...] = log
    back = jnp.zeros((64, 128), F32)
    for j in range(2):
        for p in pieces(log):
            back = back + mm((los[j] * p.astype(F32)).astype(BF16), his[j], NT)
    for k in range(CHUNKS):
        col = jnp.sum(jnp.where(lanes == 4 * k + me, back, 0.0), axis=1, keepdims=True)
        w_ref[k, me] = jnp.exp(total_ref[k] - col).astype(BF16)

    def own(k):
        return (
            ring_hop(ring2, 0, k, right, dom, w_ref.at[k, me], w_ref.at[k, me]),
            ring_hop(ring2, 1, k, left, dom, w_ref.at[k, me], w_ref.at[k, me]),
        )

    def forward(k):
        return (
            ring_hop(ring2, 2, k, right, dom, w_ref.at[k, left, low], w_ref.at[k, left, low]),
            ring_hop(ring2, 3, k, left, dom, w_ref.at[k, right, high], w_ref.at[k, right, high]),
        )

    def begin(copies):
        for c in copies:
            c.start()

    def end(copies):
        for c in copies:
            c.wait()

    for k in range(3):
        begin(own(k))
    end(own(0))
    begin(forward(0))
    s_col = iota((SLOTS, PAIRS), 0)
    k_col = iota((8, 128), 0) + me * 8
    fold = folds()

    def spread_out(pair, u, raw):
        g = pair * 2 + u
        at = tab_ref[g, SLOTS]
        w = jnp.concatenate([wide[at + j] for j in range(8)], axis=0)
        w = jnp.where(s_col < tab_ref[g, SLOTS + 1], w, 0.0)
        wt = jnp.transpose(w).astype(BF16)
        for n in range(4):
            at = slice(n * 256, (n + 1) * 256)
            raw[:, at] = mm(wt, wall[g, :, at]).astype(BF16)
        kinds = kinds_ref[pl.ds(g, 1), :]
        hit = onehot(k_col == kinds)[:, 0:SLOTS]
        pk = mm(hit, w.astype(BF16))
        msg[g, 32:48, :] = jnp.concatenate([pk[:, 0:128], pk[:, 128:256]], axis=0).astype(BF16)

    def fold_pair(pair):
        out = folded([parts[h] for h in range(2)], fold).astype(BF16)
        for u in range(2):
            msg[pair * 2 + u, 0:32, :] = out[u * 32 : (u + 1) * 32, :]

    def to_owner(i):
        return pltpu.make_async_remote_copy(
            src_ref=msg.at[i],
            dst_ref=got.at[i],
            send_sem=ssem.at[i],
            recv_sem=rsem.at[i],
            device_id=(me, owner_of(dom, i)),
            device_id_type=MESH,
        )

    def step(t, _):
        @pl.when(t > 4)
        def _():
            to_owner(2 * (t - 4)).start()

        @pl.when(t > 3)
        def _():
            to_owner(2 * (t - 4) + 1).start()

        fold_pair(jnp.clip(t - 3, 0, PAIRS_OF - 1))
        for u in range(2):
            diag = diagonal(rott_ref, rsqs[u])
            for h in range(2):
                parts[h, u * 32 : (u + 1) * 32, :] = diag[h * 32 : (h + 1) * 32, :]
        for u in range(2):
            turned(raws[u], rsqs[u])
        for u in range(2):
            spread_out(jnp.minimum(t, PAIRS_OF - 1), u, raws[u])
        return 0

    def chunk(k, _):
        @pl.when(k + 3 < CHUNKS)
        def _():
            begin(own(k + 3))

        @pl.when(k + 1 < CHUNKS)
        def _():
            end(own(k + 1))
            begin(forward(k + 1))

        end(forward(k))
        for q in range(SHARES):
            wide[pl.ds(k * 32 + q * 8, 8)] = w_ref[k, q].astype(F32).reshape(8, 8, PAIRS)
        lax.fori_loop(2 * k, 2 * k + 2, step, 0)
        return 0

    lax.fori_loop(0, CHUNKS, chunk, 0)
    lax.fori_loop(2 * CHUNKS, PAIRS_OF + 3, step, 0)
    for u in range(2):
        to_owner(GROUPS - 2 + u).start()

    def arrive(i, acc):
        to_owner(i).wait()
        return acc + got[i].astype(F32)

    acc = lax.fori_loop(1, GROUPS, arrive, msg[0].astype(F32))
    mine[...] = acc[32:48, :]
    shares = [to_peer(share_sem, d, mine, others.at[d - 1]) for d in range(1, SHARES)]
    for c in shares:
        c.start()

    sums_ref[...] = acc[0:32, :]
    for c in shares:
        c.wait()
    rows = []
    for k in range(SHARES):
        x = mine[...]
        for d in range(1, SHARES):
            x = jnp.where(lax.rem(k + d, SHARES) == me, others[d - 1], x)
        rows.append(jnp.concatenate([x[0:8, :], x[8:16, :]], axis=1))
    pk_ref[...] = jnp.concatenate(rows, axis=0)


def last_kernel(sums_ref, pk_ref, log_in, ctf_ref, rott_ref, cs_ref, cw_ref, log_ref, raw, rsq, placing):
    def placed(x, ref):
        placing[:, 0:32] = jnp.transpose(x)
        for l in range(CYC):
            piece = [placing[pl.ds(h * 64 + l, CPG, stride=CYC), 0:32] for h in range(2)]
            ref[:, l * ANG : (l + 1) * ANG] = jnp.concatenate(piece, axis=1).astype(ref.dtype)

    for j in range(8):
        log_ref[j : j + 1, :] = log_in[:, j * 128 : (j + 1) * 128]
    placed(sums_ref[...], cs_ref)
    pkt = jnp.transpose(pk_ref[...])
    power = ctf_ref[...] * ctf_ref[...]
    for n in range(4):
        at = slice(n * 256, (n + 1) * 256)
        raw[:, at] = lax.dot_general(
            pkt, power[:, at], NN, precision=lax.Precision.HIGHEST, preferred_element_type=F32
        ).astype(BF16)
    turned(raw, rsq)
    diag = diagonal(rott_ref, rsq)
    placed(folded([diag[0:32], diag[32:64]], folds()), cw_ref)


def last_stage(sums, pk, log, ctf, rott):
    return pl.pallas_call(
        last_kernel,
        out_shape=(
            jax.ShapeDtypeStruct((CPG, PIX), BF16),
            jax.ShapeDtypeStruct((CPG, PIX), F32),
            jax.ShapeDtypeStruct((8, TOK // 8), F32),
        ),
        in_specs=vm(5),
        out_specs=tuple(vm(3)),
        scratch_shapes=[
            pltpu.VMEM((PAIRS, PIX), BF16),
            pltpu.VMEM((1024, 256), BF16),
            pltpu.VMEM((128, 128), F32),
        ],
        compiler_params=pltpu.CompilerParams(vmem_limit_bytes=VMEM_LIMIT),
        name="last_stage",
    )(sums, pk, log, ctf, rott)


def main_stage(tab, packing, xs, refs, rott, ctf, kinds, rho):
    return pl.pallas_call(
        main_kernel,
        out_shape=(
            jax.ShapeDtypeStruct((32, 128), F32),
            jax.ShapeDtypeStruct((KINDS, PAIRS), F32),
            jax.ShapeDtypeStruct((1, TOK), F32),
        ),
        in_specs=[pl.BlockSpec(memory_space=pltpu.SMEM)] * 2 + vm(6),
        out_specs=tuple(vm(3)),
        scratch_shapes=[
            pltpu.VMEM((KINDS, 8, 128), F32),
            pltpu.VMEM((64, PIX), BF16),
            pltpu.VMEM((512, 256), BF16),
            pltpu.VMEM((512, PIX), BF16),
            pltpu.VMEM((PIX, PAIRS), BF16),
            pltpu.VMEM((PIX, PAIRS), BF16),
            pltpu.VMEM((SLOTS * 8, 128), F32),
            pltpu.VMEM((SLOTS * 8, 128), F32),
            pltpu.VMEM((SLOTS, 128), BF16),
            pltpu.VMEM((SLOTS, 128), BF16),
            pltpu.VMEM((GROUPS, SLOTS, PIX), BF16),
            pltpu.VMEM((GROUPS * 8, 8, PAIRS), F32),
            pltpu.VMEM((CHUNKS, SHARES, 64, PAIRS), F32),
            pltpu.VMEM((CHUNKS, 2, 32, PAIRS), F32),
            pltpu.VMEM((CHUNKS, 2, 32, PAIRS), F32),
            pltpu.VMEM((CHUNKS, 2, 64, PAIRS), F32),
            pltpu.VMEM((CHUNKS, 64, PAIRS), F32),
            pltpu.VMEM((CHUNKS, SHARES, 64, PAIRS), BF16),
            pltpu.VMEM((PACKED // 8, 8, PAIRS), F32),
            pltpu.VMEM((2, 64, 128), F32),
            pltpu.VMEM((SHARES - 1, 2, 64, 128), F32),
            pltpu.VMEM((1024, 256), BF16),
            pltpu.VMEM((1024, 256), BF16),
            pltpu.VMEM((PAIRS, PIX), BF16),
            pltpu.VMEM((PAIRS, PIX), BF16),
            pltpu.VMEM((2, 64, 256), F32),
            pltpu.VMEM((GROUPS, 48, 128), BF16),
            pltpu.VMEM((GROUPS, 48, 128), BF16),
            pltpu.VMEM((16, 128), F32),
            pltpu.VMEM((SHARES - 1, 16, 128), F32),
            pltpu.SemaphoreType.DMA((2, 6, CHUNKS)),
            pltpu.SemaphoreType.DMA((2, 4, CHUNKS)),
            pltpu.SemaphoreType.DMA((2, SHARES)),
            pltpu.SemaphoreType.DMA((GROUPS,)),
            pltpu.SemaphoreType.DMA((GROUPS,)),
            pltpu.SemaphoreType.DMA((2, SHARES)),
        ],
        compiler_params=pltpu.CompilerParams(collective_id=1, has_side_effects=True, vmem_limit_bytes=VMEM_LIMIT),
        name="main_stage",
    )(tab, packing, xs.reshape(TOK, 8, 128), refs.reshape(GROUPS, 32, 128), rott, ctf, kinds, rho)


def prepared(candidates, defocus, ctf_table, references, rotations):
    mine = references.reshape(2, 2, CYC, ANG).transpose(1, 2, 0, 3).reshape(32, 128)
    rott = rotations.reshape(ROT, CYC, 4 * ANG).transpose(2, 1, 0).reshape(256, 1024)
    ctf = ctf_table.reshape(KINDS, CYC, ANG).transpose(0, 2, 1).reshape(KINDS, PIX)
    return mine, rott, ctf, candidates.T, defocus.reshape(1, TOK)


def local(particles, candidates, defocus, ctf_table, references, rotations):
    mine, rott, ctf, cand_t, kinds_row = prepared(candidates, defocus, ctf_table, references, rotations)
    tab, kinds, rho, packing, refs, xs = start_stage(cand_t, kinds_row, mine, particles)
    sums, pk, log = main_stage(tab, packing, xs, refs, rott, ctf, kinds, rho)
    cs, cw, log = last_stage(sums, pk, log, ctf, rott)
    return cs, cw, log.reshape(TOK)


def solution(mesh):
    in_specs = (P("dom", "cls"), P("dom", None), P("dom"), P(None, "cls"), P("dom", "cls"), P())
    out_specs = (P("dom", "cls"), P("dom", "cls"), P("dom"))
    return jax.shard_map(local, mesh=mesh, in_specs=in_specs, out_specs=out_specs, check_vma=False)
```

```python
import functools

import jax
import jax.numpy as jnp
from jax import lax
from jax.experimental import pallas as pl
from jax.experimental.pallas import tpu as pltpu
from jax.sharding import PartitionSpec as P

F32 = jnp.float32
BF16 = jnp.bfloat16
I32 = jnp.int32
MESH = pl.DeviceIdType.MESH
NT = (((1,), (1,)), ((), ()))
NN = (((1,), (0,)), ((), ()))

GROUPS = 64
SLOTS = 64
ANG = 64
CYC = 16
CPG = 4
ROT = 64
PAIRS = CPG * ROT
PIX = CYC * ANG
KINDS = 32
TOK = 1024
SHARES = 4
ROWS = 640
PACKED = SHARES * ROWS
CHUNKS = ROWS // 64
PAIRS_OF = GROUPS // 2
Z, X = 8, 4
VMEM_LIMIT = 60 * 1024 * 1024


def mm(a, b, dims=NN):
    return lax.dot_general(a, b, dims, preferred_element_type=F32)


def iota(shape, dim):
    return lax.broadcasted_iota(I32, shape, dim)


def pieces(x):
    p1 = x.astype(BF16)
    r1 = x - p1.astype(F32)
    p2 = r1.astype(BF16)
    p3 = (r1 - p2.astype(F32)).astype(BF16)
    return p1, p2, p3


def onehot(mask):
    return jnp.where(mask, 1.0, 0.0).astype(BF16)


def owner_of(dom, i):
    return lax.rem(dom + (i % 8) * 8 + i // 8, GROUPS)


def vm(n):
    return [pl.BlockSpec(memory_space=pltpu.VMEM)] * n


def route(me, cand_ref, kind_ref, tab_ref, kinds_ref, rho_ref, pack_ref):
    g_iota = iota((GROUPS, TOK), 0)
    tri = onehot(iota((256, 256), 0) < iota((256, 256), 1))
    count = jnp.zeros((GROUPS, 1), F32)
    owners, ranks = [], []
    for j in range(2):
        shift = (cand_ref[j : j + 1, :] - me) & (GROUPS - 1)
        owner = onehot(g_iota == ((shift & 7) * 8 + lax.shift_right_logical(shift, 3)))
        owners.append(owner)
        row = []
        for blk in range(TOK // 256):
            part = owner[:, blk * 256 : (blk + 1) * 256]
            before = mm(part, tri) + count
            row.append(jnp.sum(before * part.astype(F32), axis=0, keepdims=True))
            count = count + jnp.sum(part.astype(F32), axis=1, keepdims=True)
        ranks.append(jnp.concatenate(row, axis=1))
    padded = jnp.floor((count + 7.0) * 0.125) * 8.0
    low = onehot(iota((GROUPS, GROUPS), 1) < iota((GROUPS, GROUPS), 0))
    offset = mm(low, jnp.broadcast_to(padded, (GROUPS, 128)).astype(BF16))[:, 0:1]
    at = iota((GROUPS, 384), 1) * 8
    ended = jnp.where(at >= (offset + padded).astype(I32), 1, 0)
    where_in = jnp.sum(ended, axis=0, keepdims=True)
    first = jnp.sum(jnp.where(iota((GROUPS, 384), 0) == where_in, offset.astype(I32), 0), axis=0, keepdims=True)
    source = where_in * 8 + (iota((1, 384), 1) - lax.shift_right_logical(first, 3))
    pack_ref[...] = jnp.where(where_in < GROUPS, source, 0)
    tok = iota((1, TOK), 1)
    s_iota = iota((SLOTS, TOK), 0)
    high = jnp.zeros((GROUPS, SLOTS), F32)
    low_part = jnp.zeros((GROUPS, SLOTS), F32)
    for j in range(2):
        slot = onehot(s_iota == ranks[j].astype(I32))
        v1 = (tok // 8).astype(F32)
        v2 = ((tok % 8) * 32 + kind_ref[...]).astype(F32)
        high = high + mm(owners[j], (slot.astype(F32) * v1).astype(BF16), NT)
        low_part = low_part + mm(owners[j], (slot.astype(F32) * v2).astype(BF16), NT)
        at = jnp.sum(owners[j].astype(F32) * offset, axis=0, keepdims=True) + ranks[j]
        rho_ref[j : j + 1, :] = at.astype(I32)
    low_int = low_part.astype(I32)
    kinds = low_int % 32
    token = high.astype(I32) * 8 + low_int // 32
    s_lane = iota((GROUPS, SLOTS), 1)
    live = s_lane < count.astype(I32)
    tab_ref[:, 0:SLOTS] = token + 1024 * kinds
    extra = jnp.where(s_lane == 0, offset * 0.125, count)
    tab_ref[:, SLOTS : 2 * SLOTS] = extra.astype(I32)
    kinds_ref[:, 0:SLOTS] = jnp.where(live, kinds, -1)
    kinds_ref[:, SLOTS : 2 * SLOTS] = jnp.full((GROUPS, SLOTS), -1, I32)


def make_perm(perm):
    def cycle(i, _):
        hit = iota((64, PIX), 1) == iota((64, PIX), 0) * CYC + i
        perm[pl.ds(pl.multiple_of(i * 64, 64), 64), :] = onehot(hit)
        return 0

    lax.fori_loop(0, CYC, cycle, 0)


def turn_pixels(part_ref, xs_ref, perm, begin, end):
    def turn_rows(i, _):
        y = mm(part_ref[pl.ds(pl.multiple_of(i * 128, 128), 128), :], perm[...])
        for j in range(8):
            xs_ref[pl.ds(i * 1024 + j, 128, stride=8), :] = y[:, j * 128 : (j + 1) * 128]
        return 0

    lax.fori_loop(begin, end, turn_rows, 0)


def start_kernel(cand_ref, kind_ref, own_refs, part_ref, ctf_ref, tab_ref, kinds_ref, rho_ref, pack_ref, all_ref, xs_ref, ctf_out, perm, build, mine_ref, send_sem, recv_sem, own_sem):
    me = lax.axis_index("dom")
    row = lax.axis_index("cls")
    z, x, core = me // 8, (me // 2) % X, me % 2

    def peer(n):
        if n < 7:
            return lax.rem(z + n + 1, Z) * 8 + x * 2 + core
        if n < 10:
            return z * 8 + lax.rem(x + n - 6, X) * 2 + core
        return z * 8 + x * 2 + (1 - core)

    barrier = pltpu.get_barrier_semaphore()
    for n in range(11):
        pl.semaphore_signal(barrier, inc=1, device_id=(row, peer(n)), device_id_type=MESH)
    refs = own_refs[...].astype(F32)
    for c in range(CPG):
        for l in range(CYC):
            r = (c % 2) * CYC + l
            build[r : r + 1, (c // 2) * ANG : (c // 2 + 1) * ANG] = refs[c : c + 1, l * ANG : (l + 1) * ANG]
    mine_ref[...] = build[...].astype(BF16)
    route(me, cand_ref, kind_ref, tab_ref, kinds_ref, rho_ref, pack_ref)
    make_perm(perm)
    pl.semaphore_wait(barrier, 11)

    def copy(n):
        if n < 7:
            src, dst = mine_ref, all_ref.at[z, x, core]
        elif n < 10:
            src = dst = all_ref.at[:, x, core]
        else:
            src = dst = all_ref.at[:, :, core]
        return pltpu.make_async_remote_copy(
            src_ref=src,
            dst_ref=dst,
            send_sem=send_sem.at[n],
            recv_sem=recv_sem.at[n],
            device_id=(row, peer(n)),
            device_id_type=MESH,
        )

    first = [copy(n) for n in range(7)]
    second = [copy(n) for n in range(7, 10)]
    third = copy(10)
    for c in first:
        c.start()
    own = pltpu.make_async_copy(mine_ref, all_ref.at[z, x, core], own_sem)
    own.start()
    y = mm(jnp.concatenate(list(pieces(ctf_ref[...])), axis=0), perm[...])
    ctf_out[...] = y[0:KINDS] + y[KINDS : 2 * KINDS] + y[2 * KINDS : 3 * KINDS]
    turn_pixels(part_ref, xs_ref, perm, 0, 4)
    own.wait()
    for c in first:
        c.wait()
    for c in second:
        c.start()
    turn_pixels(part_ref, xs_ref, perm, 4, 7)
    for c in second:
        c.wait()
    third.start()
    turn_pixels(part_ref, xs_ref, perm, 7, 8)
    third.wait()


def start_stage(cand_t, kinds_row, references, particles, ctf_table):
    return pl.pallas_call(
        start_kernel,
        out_shape=(
            jax.ShapeDtypeStruct((GROUPS, 2 * SLOTS), I32),
            jax.ShapeDtypeStruct((GROUPS, 2 * SLOTS), I32),
            jax.ShapeDtypeStruct((2, TOK), I32),
            jax.ShapeDtypeStruct((1, 384), I32),
            jax.ShapeDtypeStruct((Z, X, 2, 32, 128), BF16),
            jax.ShapeDtypeStruct((TOK * 8, 128), F32),
            jax.ShapeDtypeStruct((KINDS, PIX), F32),
        ),
        in_specs=vm(5),
        out_specs=tuple(vm(7)),
        scratch_shapes=[
            pltpu.VMEM((PIX, PIX), BF16),
            pltpu.VMEM((32, 128), F32),
            pltpu.VMEM((32, 128), BF16),
            pltpu.SemaphoreType.DMA((11,)),
            pltpu.SemaphoreType.DMA((11,)),
            pltpu.SemaphoreType.DMA,
        ],
        compiler_params=pltpu.CompilerParams(collective_id=0, has_side_effects=True, vmem_limit_bytes=VMEM_LIMIT),
        name="start_stage",
    )(cand_t, kinds_row, references, particles, ctf_table)


def turned(raw, rsq):
    keep = jnp.broadcast_to(iota((1, 128), 1) < 64, (64, 128))
    for qp in range(8):
        for c in range(2):
            a = raw[c * 128 : c * 128 + 64, qp * 128 : (qp + 1) * 128]
            b = raw[c * 128 + 64 : c * 128 + 128, qp * 128 : (qp + 1) * 128]
            e = jnp.where(keep, a, pltpu.roll(b, 64, 1))
            o = jnp.where(keep, pltpu.roll(a, 64, 1), b)
            rsq[qp * 128 : qp * 128 + 64, c * 128 : (c + 1) * 128] = e
            rsq[qp * 128 + 64 : qp * 128 + 128, c * 128 : (c + 1) * 128] = o


def diagonal(rott_ref, rsq):
    lane = iota((1, 256), 1)
    total = None
    for part in range(2):
        at = slice(part * 512, (part + 1) * 512)
        full = mm(rott_ref[:, at], rsq[at, :])
        diag = full[0:64, :]
        for b in range(1, 4):
            diag = jnp.where((lane // CYC) % 4 == b, full[b * 64 : (b + 1) * 64, :], diag)
        total = diag if total is None else total + diag
    return total


def folds():
    ri = iota((256, 128), 0)
    ci = iota((256, 128), 1)
    want = (ri // 64) * CYC + ri % CYC
    return [onehot(ci == want + 64 * h) for h in range(2)]


def folded(parts, fold):
    out = None
    for x, f in zip(parts, fold):
        p1 = x.astype(BF16)
        p2 = (x - p1.astype(F32)).astype(BF16)
        y = mm(p1, f) + mm(p2, f)
        out = y if out is None else out + y
    return out


def ring_hop(ring, n, k, to, dom, src, dst):
    return pltpu.make_async_remote_copy(
        src_ref=src,
        dst_ref=dst,
        send_sem=ring.at[0, n, k],
        recv_sem=ring.at[1, n, k],
        device_id=(to, dom),
        device_id_type=MESH,
    )


def main_kernel(tab_ref, pack_ref, xs, refs_ref, rott_ref, ctf_ref, kinds_ref, rho_ref, sums_ref, pk_ref, log_ref, cs, power, bd, raw, rot_a, rot_b, stage_a, stage_b, hits_a, hits_b, weights_a, weights_b, wall, table, packed, far, held, near, total_ref, w_ref, wide, stat, stat_recv, rsq_a, rsq_b, raw_a, raw_b, parts, msg, got, mine, others, ring, ring2, stat_sem, ssem, rsem, share_sem):
    rots, stages, hits = (rot_a, rot_b), (stage_a, stage_b), (hits_a, hits_b)
    rsqs, raws = (rsq_a, rsq_b), (raw_a, raw_b)
    weights = (weights_a, weights_b)
    me = lax.axis_index("cls")
    dom = lax.axis_index("dom")
    right, left, across = lax.rem(me + 1, SHARES), lax.rem(me + 3, SHARES), lax.rem(me + 2, SHARES)
    low, high = pl.ds(0, 32), pl.ds(32, 32)
    barrier = pltpu.get_barrier_semaphore()
    for d in range(1, SHARES):
        pl.semaphore_signal(barrier, inc=1, device_id=(lax.rem(me + d, SHARES), dom), device_id_type=MESH)

    def greet(i, _):
        pl.semaphore_signal(barrier, inc=1, device_id=(me, lax.rem(dom + i, GROUPS)), device_id_type=MESH)
        return 0

    lax.fori_loop(1, GROUPS, greet, 0)

    def outgoing(k):
        return (
            ring_hop(ring, 0, k, right, dom, packed.at[k, across, low], far.at[k, 0]),
            ring_hop(ring, 1, k, left, dom, packed.at[k, across, high], far.at[k, 1]),
            ring_hop(ring, 2, k, right, dom, packed.at[k, right, high], near.at[k, 0, high]),
            ring_hop(ring, 3, k, left, dom, packed.at[k, left, low], near.at[k, 1, low]),
        )

    def relayed(k):
        return (
            ring_hop(ring, 4, k, right, dom, held.at[k, 0], near.at[k, 0, low]),
            ring_hop(ring, 5, k, left, dom, held.at[k, 1], near.at[k, 1, high]),
        )

    def pack(k):
        for q in range(SHARES):
            for j in range(8):
                src = pack_ref[0, k * 32 + q * 8 + j]
                packed[k, q, j * 8 : (j + 1) * 8, :] = table[src]
        for c in outgoing(k):
            c.start()

    def relay(k):
        c0, c1, _, _ = outgoing(k)
        c0.wait()
        c1.wait()
        held[k, 0] = packed[k, right, low, :] + far[k, 0]
        held[k, 1] = packed[k, left, high, :] + far[k, 1]
        for c in relayed(k):
            c.start()

    for j in range(8):
        cs[:, j, :] = ctf_ref[:, j * 128 : (j + 1) * 128]
    square = -0.5 * (ctf_ref[...] * ctf_ref[...])
    s1 = square.astype(BF16)
    power[0:32, :] = s1
    power[32:64, :] = (square - s1.astype(F32)).astype(BF16)
    bd[...] = jnp.zeros_like(bd)
    half = iota((1, 128), 1) < 64
    keep = jnp.broadcast_to(half, (64, 128))
    keep_16 = jnp.broadcast_to(half, (16, 128))
    blank = jnp.zeros((16, 128), BF16)
    k_row = iota((128, 128), 0)

    def rotate(pair):
        for u in range(2):
            for cl in range(2):
                x = refs_ref[owner_of(dom, pair * 2 + u), cl * 16 : (cl + 1) * 16, :]
                y = pltpu.roll(x, 64, 1)
                for ch, (low, high) in enumerate(((x, y), (y, x))):
                    at = u * 256 + (ch * 2 + cl) * 64
                    low = jnp.where(keep_16, low, blank)
                    high = jnp.where(keep_16, blank, high)
                    bd[at : at + 16, 0:128] = low
                    bd[at + 16 : at + 32, 0:128] = high
                    bd[at + 32 : at + 48, 128:256] = low
                    bd[at + 48 : at + 64, 128:256] = high
        for n in range(4):
            at = slice(n * 256, (n + 1) * 256)
            raw[:, at] = mm(bd[...], rott_ref[:, at]).astype(BF16)

    def arrange(pair, u):
        g = pair * 2 + u
        rot, stage = rots[u], stages[u]
        for s in range(SLOTS):
            entry = tab_ref[g, s]
            stage[s * 8 : (s + 1) * 8, :] = xs[entry & 1023] * cs[lax.shift_right_logical(entry, 10)]
        for qp in range(8):
            for k in range(2):
                r0 = u * 256 + k * 128
                a = raw[r0 : r0 + 64, qp * 128 : (qp + 1) * 128]
                b = raw[r0 + 64 : r0 + 128, qp * 128 : (qp + 1) * 128]
                rot[qp * 128 : qp * 128 + 64, k * 128 : (k + 1) * 128] = jnp.where(keep, a, pltpu.roll(b, 64, 1))
                rot[qp * 128 + 64 : qp * 128 + 128, k * 128 : (k + 1) * 128] = jnp.where(keep, pltpu.roll(a, 64, 1), b)
        for j in range(8):
            col = stage[pl.ds(j, SLOTS, stride=8), :].astype(BF16)
            wall[g, :, j * 128 : (j + 1) * 128] = col
            weights[u][:, j * 128 : (j + 1) * 128] = col
        kinds = kinds_ref[pl.ds(g, 1), :]
        hit = jnp.where(((k_row & 31) == kinds) & (k_row < 64), 1.0, 0.0)
        hits[u][...] = jnp.transpose(hit)[0:SLOTS, :].astype(BF16)

    def score(pair, u):
        g = pair * 2 + u
        rot = rots[u]
        en, total = None, None
        for part in range(2):
            at = slice(part * 512, (part + 1) * 512)
            r = rot[at, :]
            z = mm(weights[u][:, at], r)
            y = mm(power[:, at], r * r)
            total = z if total is None else total + z
            en = y if en is None else en + y
        en = en[0:32, :] + en[32:64, :]
        p1 = en.astype(BF16)
        p2 = (en - p1.astype(F32)).astype(BF16)
        total = total + mm(hits[u][:, 0:64], jnp.concatenate([p1, p2], axis=0))
        table[pl.ds(g * 8, 8)] = (total * (4.0 / 64.0)).reshape(8, 8, PAIRS)

    def step(t, _):
        for u in range(2):
            score(jnp.clip(t - 2, 0, PAIRS_OF - 1), u)
        for u in range(2):
            arrange(jnp.clip(t - 1, 0, PAIRS_OF - 1), u)
        rotate(jnp.minimum(t, PAIRS_OF - 1))
        return 0

    lax.fori_loop(0, 18, step, 0)
    pl.semaphore_wait(barrier, GROUPS - 1 + SHARES - 1)

    def chunk(k, _):
        lax.fori_loop(18 + 2 * k, 20 + 2 * k, step, 0)
        pack(k)

        @pl.when(k > 0)
        def _():
            relay(k - 1)

        return 0

    lax.fori_loop(0, 8, chunk, 0)

    pack(8)
    relay(7)
    pack(9)
    relay(8)
    relay(9)

    def finish(k, _):
        _, _, c2, c3 = outgoing(k)
        c4, c5 = relayed(k)
        for c in (c2, c3, c4, c5):
            c.wait()
        total_ref[k] = packed[k, me] + near[k, 0] + near[k, 1]
        return 0

    lax.fori_loop(0, CHUNKS, finish, 0)

    lanes = iota((64, 128), 1)
    top = jnp.zeros((64, 128), F32)
    tot = jnp.zeros((64, 128), F32)
    for k in range(CHUNKS):
        x = total_ref[k]
        m = jnp.max(x, axis=1, keepdims=True)
        s = jnp.sum(jnp.exp(x - m), axis=1, keepdims=True)
        here = lanes == 4 * k + me
        top = jnp.where(here, m, top)
        tot = jnp.where(here, s, tot)
    stat[0] = top
    stat[1] = tot
    def to_peer(sem, d, src, dst):
        return pltpu.make_async_remote_copy(
            src_ref=src,
            dst_ref=dst,
            send_sem=sem.at[0, d],
            recv_sem=sem.at[1, d],
            device_id=(lax.rem(me + d, SHARES), dom),
            device_id_type=MESH,
        )

    swaps = [to_peer(stat_sem, d, stat, stat_recv.at[d - 1]) for d in (2, 1, 3)]
    for c in swaps:
        c.start()
    his, los = [], []
    for j in range(2):
        rho = rho_ref[j : j + 1, :]
        his.append(onehot(iota((128, TOK), 0) == lax.shift_right_logical(rho, 6)))
        los.append(jnp.where(iota((64, TOK), 0) == (rho & 63), 1.0, 0.0))
    for c in swaps:
        c.wait()
    top = stat[0] + stat_recv[0, 0] + stat_recv[1, 0] + stat_recv[2, 0]
    tot = stat[1] + stat_recv[0, 1] + stat_recv[1, 1] + stat_recv[2, 1]
    three = jnp.concatenate(list(pieces(top)) + list(pieces(tot)), axis=0)
    maxima, sums = [], []
    for j in range(2):
        t = mm(three, his[j])
        maxima.append(jnp.sum((t[0:64] + t[64:128] + t[128:192]) * los[j], axis=0, keepdims=True))
        sums.append(jnp.sum((t[192:256] + t[256:320] + t[320:384]) * los[j], axis=0, keepdims=True))
    best = jnp.maximum(maxima[0], maxima[1])
    log = best + jnp.log(sums[0] * jnp.exp(maxima[0] - best) + sums[1] * jnp.exp(maxima[1] - best))
    log_ref[...] = log
    back = jnp.zeros((64, 128), F32)
    for j in range(2):
        for p in pieces(log):
            back = back + mm((los[j] * p.astype(F32)).astype(BF16), his[j], NT)
    for k in range(CHUNKS):
        col = jnp.sum(jnp.where(lanes == 4 * k + me, back, 0.0), axis=1, keepdims=True)
        w_ref[k, me] = jnp.exp(total_ref[k] - col).astype(BF16)

    def own(k):
        return (
            ring_hop(ring2, 0, k, right, dom, w_ref.at[k, me], w_ref.at[k, me]),
            ring_hop(ring2, 1, k, left, dom, w_ref.at[k, me], w_ref.at[k, me]),
        )

    def forward(k):
        return (
            ring_hop(ring2, 2, k, right, dom, w_ref.at[k, left, low], w_ref.at[k, left, low]),
            ring_hop(ring2, 3, k, left, dom, w_ref.at[k, right, high], w_ref.at[k, right, high]),
        )

    def begin(copies):
        for c in copies:
            c.start()

    def end(copies):
        for c in copies:
            c.wait()

    for k in range(3):
        begin(own(k))
    end(own(0))
    begin(forward(0))
    s_col = iota((SLOTS, PAIRS), 0)
    k_col = iota((8, 128), 0) + me * 8
    fold = folds()

    def spread_out(pair, u, raw):
        g = pair * 2 + u
        at = tab_ref[g, SLOTS]
        w = jnp.concatenate([wide[at + j] for j in range(8)], axis=0)
        w = jnp.where(s_col < tab_ref[g, SLOTS + 1], w, 0.0)
        wt = jnp.transpose(w).astype(BF16)
        for n in range(4):
            at = slice(n * 256, (n + 1) * 256)
            raw[:, at] = mm(wt, wall[g, :, at]).astype(BF16)
        kinds = kinds_ref[pl.ds(g, 1), :]
        hit = onehot(k_col == kinds)[:, 0:SLOTS]
        pk = mm(hit, w.astype(BF16))
        msg[g, 32:48, :] = jnp.concatenate([pk[:, 0:128], pk[:, 128:256]], axis=0).astype(BF16)

    def fold_pair(pair):
        out = folded([parts[h] for h in range(2)], fold).astype(BF16)
        for u in range(2):
            msg[pair * 2 + u, 0:32, :] = out[u * 32 : (u + 1) * 32, :]

    def to_owner(i):
        return pltpu.make_async_remote_copy(
            src_ref=msg.at[i],
            dst_ref=got.at[i],
            send_sem=ssem.at[i],
            recv_sem=rsem.at[i],
            device_id=(me, owner_of(dom, i)),
            device_id_type=MESH,
        )

    def step(t, _):
        @pl.when(t > 4)
        def _():
            to_owner(2 * (t - 4)).start()

        @pl.when(t > 3)
        def _():
            to_owner(2 * (t - 4) + 1).start()

        fold_pair(jnp.clip(t - 3, 0, PAIRS_OF - 1))
        for u in range(2):
            diag = diagonal(rott_ref, rsqs[u])
            for h in range(2):
                parts[h, u * 32 : (u + 1) * 32, :] = diag[h * 32 : (h + 1) * 32, :]
        for u in range(2):
            turned(raws[u], rsqs[u])
        for u in range(2):
            spread_out(jnp.minimum(t, PAIRS_OF - 1), u, raws[u])
        return 0

    def chunk(k, _):
        @pl.when(k + 3 < CHUNKS)
        def _():
            begin(own(k + 3))

        @pl.when(k + 1 < CHUNKS)
        def _():
            end(own(k + 1))
            begin(forward(k + 1))

        end(forward(k))
        for q in range(SHARES):
            wide[pl.ds(k * 32 + q * 8, 8)] = w_ref[k, q].astype(F32).reshape(8, 8, PAIRS)
        lax.fori_loop(2 * k, 2 * k + 2, step, 0)
        return 0

    lax.fori_loop(0, CHUNKS, chunk, 0)
    lax.fori_loop(2 * CHUNKS, PAIRS_OF + 3, step, 0)
    for u in range(2):
        to_owner(GROUPS - 2 + u).start()

    def arrive(i, acc):
        to_owner(i).wait()
        return acc + got[i].astype(F32)

    acc = lax.fori_loop(1, GROUPS, arrive, msg[0].astype(F32))
    mine[...] = acc[32:48, :]
    shares = [to_peer(share_sem, d, mine, others.at[d - 1]) for d in range(1, SHARES)]
    for c in shares:
        c.start()

    sums_ref[...] = acc[0:32, :]
    for c in shares:
        c.wait()
    rows = []
    for k in range(SHARES):
        x = mine[...]
        for d in range(1, SHARES):
            x = jnp.where(lax.rem(k + d, SHARES) == me, others[d - 1], x)
        rows.append(jnp.concatenate([x[0:8, :], x[8:16, :]], axis=1))
    pk_ref[...] = jnp.concatenate(rows, axis=0)


def last_kernel(sums_ref, pk_ref, log_in, ctf_ref, rott_ref, cs_ref, cw_ref, log_ref, raw, rsq, placing):
    def placed(x, ref):
        placing[:, 0:32] = jnp.transpose(x)
        for l in range(CYC):
            piece = [placing[pl.ds(h * 64 + l, CPG, stride=CYC), 0:32] for h in range(2)]
            ref[:, l * ANG : (l + 1) * ANG] = jnp.concatenate(piece, axis=1).astype(ref.dtype)

    for j in range(8):
        log_ref[j : j + 1, :] = log_in[:, j * 128 : (j + 1) * 128]
    placed(sums_ref[...], cs_ref)
    pkt = jnp.transpose(pk_ref[...])
    power = ctf_ref[...] * ctf_ref[...]
    for n in range(4):
        at = slice(n * 256, (n + 1) * 256)
        raw[:, at] = lax.dot_general(
            pkt, power[:, at], NN, precision=lax.Precision.HIGHEST, preferred_element_type=F32
        ).astype(BF16)
    turned(raw, rsq)
    diag = diagonal(rott_ref, rsq)
    placed(folded([diag[0:32], diag[32:64]], folds()), cw_ref)


def last_stage(sums, pk, log, ctf, rott):
    return pl.pallas_call(
        last_kernel,
        out_shape=(
            jax.ShapeDtypeStruct((CPG, PIX), BF16),
            jax.ShapeDtypeStruct((CPG, PIX), F32),
            jax.ShapeDtypeStruct((8, TOK // 8), F32),
        ),
        in_specs=vm(5),
        out_specs=tuple(vm(3)),
        scratch_shapes=[
            pltpu.VMEM((PAIRS, PIX), BF16),
            pltpu.VMEM((1024, 256), BF16),
            pltpu.VMEM((128, 128), F32),
        ],
        compiler_params=pltpu.CompilerParams(vmem_limit_bytes=VMEM_LIMIT),
        name="last_stage",
    )(sums, pk, log, ctf, rott)


def main_stage(tab, packing, xs, refs, rott, ctf, kinds, rho):
    return pl.pallas_call(
        main_kernel,
        out_shape=(
            jax.ShapeDtypeStruct((32, 128), F32),
            jax.ShapeDtypeStruct((KINDS, PAIRS), F32),
            jax.ShapeDtypeStruct((1, TOK), F32),
        ),
        in_specs=[pl.BlockSpec(memory_space=pltpu.SMEM)] * 2 + vm(6),
        out_specs=tuple(vm(3)),
        scratch_shapes=[
            pltpu.VMEM((KINDS, 8, 128), F32),
            pltpu.VMEM((64, PIX), BF16),
            pltpu.VMEM((512, 256), BF16),
            pltpu.VMEM((512, PIX), BF16),
            pltpu.VMEM((PIX, PAIRS), BF16),
            pltpu.VMEM((PIX, PAIRS), BF16),
            pltpu.VMEM((SLOTS * 8, 128), F32),
            pltpu.VMEM((SLOTS * 8, 128), F32),
            pltpu.VMEM((SLOTS, 128), BF16),
            pltpu.VMEM((SLOTS, 128), BF16),
            pltpu.VMEM((SLOTS, PIX), BF16),
            pltpu.VMEM((SLOTS, PIX), BF16),
            pltpu.VMEM((GROUPS, SLOTS, PIX), BF16),
            pltpu.VMEM((GROUPS * 8, 8, PAIRS), F32),
            pltpu.VMEM((CHUNKS, SHARES, 64, PAIRS), F32),
            pltpu.VMEM((CHUNKS, 2, 32, PAIRS), F32),
            pltpu.VMEM((CHUNKS, 2, 32, PAIRS), F32),
            pltpu.VMEM((CHUNKS, 2, 64, PAIRS), F32),
            pltpu.VMEM((CHUNKS, 64, PAIRS), F32),
            pltpu.VMEM((CHUNKS, SHARES, 64, PAIRS), BF16),
            pltpu.VMEM((PACKED // 8, 8, PAIRS), F32),
            pltpu.VMEM((2, 64, 128), F32),
            pltpu.VMEM((SHARES - 1, 2, 64, 128), F32),
            pltpu.VMEM((1024, 256), BF16),
            pltpu.VMEM((1024, 256), BF16),
            pltpu.VMEM((PAIRS, PIX), BF16),
            pltpu.VMEM((PAIRS, PIX), BF16),
            pltpu.VMEM((2, 64, 256), F32),
            pltpu.VMEM((GROUPS, 48, 128), BF16),
            pltpu.VMEM((GROUPS, 48, 128), BF16),
            pltpu.VMEM((16, 128), F32),
            pltpu.VMEM((SHARES - 1, 16, 128), F32),
            pltpu.SemaphoreType.DMA((2, 6, CHUNKS)),
            pltpu.SemaphoreType.DMA((2, 4, CHUNKS)),
            pltpu.SemaphoreType.DMA((2, SHARES)),
            pltpu.SemaphoreType.DMA((GROUPS,)),
            pltpu.SemaphoreType.DMA((GROUPS,)),
            pltpu.SemaphoreType.DMA((2, SHARES)),
        ],
        compiler_params=pltpu.CompilerParams(collective_id=1, has_side_effects=True, vmem_limit_bytes=VMEM_LIMIT),
        name="main_stage",
    )(tab, packing, xs.reshape(TOK, 8, 128), refs.reshape(GROUPS, 32, 128), rott, ctf, kinds, rho)


def local(particles, candidates, defocus, ctf_table, references, rotations):
    rott = rotations.reshape(ROT, CYC, 4 * ANG).transpose(2, 1, 0).reshape(256, 1024)
    tab, kinds, rho, packing, refs, xs, ctf = start_stage(
        candidates.T, defocus.reshape(1, TOK), references, particles, ctf_table
    )
    sums, pk, log = main_stage(tab, packing, xs, refs, rott, ctf, kinds, rho)
    cs, cw, log = last_stage(sums, pk, log, ctf, rott)
    return cs, cw, log.reshape(TOK)


def solution(mesh):
    in_specs = (P("dom", "cls"), P("dom", None), P("dom"), P(None, "cls"), P("dom", "cls"), P())
    out_specs = (P("dom", "cls"), P("dom", "cls"), P("dom"))
    return jax.shard_map(local, mesh=mesh, in_specs=in_specs, out_specs=out_specs, check_vma=False)
```
